32 devices in a mesh: dp: 8 (over z, y), tensor: 4 (over x, core).
Axes of the slice: x: 2, y: 2, z: 4, core: 2. Of those that a mesh axis runs over, the one named last changes fastest.
Arguments:
- tokens: bfloat16 [8224, 1024], P('dp', 'tensor'), may hold values from -6 to 6
- norm1_gain: float32 [1024], replicated, may hold values from 0.25 to 1.75
- norm1_bias: float32 [1024], replicated, may hold values from -3 to 3
- qkv_weight: bfloat16 [1024, 3072], P(None, 'tensor'), may hold values from -0.1875 to 0.1875
- query_bias: float32 [1024], P('tensor'), may hold values from -3 to 3
- value_bias: float32 [1024], P('tensor'), may hold values from -3 to 3
- out_weight: bfloat16 [1024, 1024], P('tensor'), may hold values from -1.5 to 1.5
- out_bias: float32 [1024], replicated, may hold values from -2 to 2
- layer_scale1: float32 [1024], replicated, may hold values from 0.25 to 2.5
- norm2_gain: float32 [1024], replicated, may hold values from 0.25 to 1.75
- norm2_bias: float32 [1024], replicated, may hold values from -3 to 3
- up_weight: bfloat16 [1024, 4096], P(None, 'tensor'), may hold values from -0.1875 to 0.1875
- up_bias: float32 [4096], P('tensor'), may hold values from -3 to 3
- down_weight: bfloat16 [4096, 1024], P('tensor'), may hold values from -0.09375 to 0.09375
- down_bias: float32 [1024], P('tensor'), may hold values from -2 to 2
- layer_scale2: float32 [1024], P('tensor'), may hold values from 0.25 to 2.5
- cotangent: bfloat16 [8224, 1024], P('dp', 'tensor'), may hold values from -6 to 6
Outputs:
- output: float32 [8224, 1024], P('dp', 'tensor')
- input_grad: float32 [8224, 1024], P('dp', 'tensor')
- grad_norm1_gain: float32 [1024], replicated
- grad_norm1_bias: float32 [1024], replicated
- grad_qkv_weight: float32 [1024, 3072], P(None, 'tensor')
- grad_query_bias: float32 [1024], P('tensor')
- grad_value_bias: float32 [1024], P('tensor')
- grad_out_weight: float32 [1024, 1024], P('tensor')
- grad_out_bias: float32 [1024], replicated
- grad_layer_scale1: float32 [1024], replicated
- grad_norm2_gain: float32 [1024], replicated
- grad_norm2_bias: float32 [1024], replicated
- grad_up_weight: float32 [1024, 4096], P(None, 'tensor')
- grad_up_bias: float32 [4096], P('tensor')
- grad_down_weight: float32 [4096, 1024], P('tensor')
- grad_down_bias: float32 [1024], P('tensor')
- grad_layer_scale2: float32 [1024], P('tensor')
The draws below stay inside these ranges and needn't reach their ends.
All inputs are finite; a program needn't handle non-finite values.
Results may differ from the reference program's by a relative error of at most 0.02.
Values may be sent and summed in bfloat16 or wider, within the bound.
No kernel may reach another device: no remote copies, remote signals or barrier semaphores. Data moves between devices by JAX's collectives and lax.ppermute only.
A program may use at most 128 MiB of HBM per device.

```python
import math
import jax
import jax.numpy as jnp
from jax import lax

D = 1024
H = 16
HD = 64
FF = 4096
TOK_IMG = 257
TOKENS = 8224
N_TENSOR = 4


def level_of(stream_key, shape, split, least, high):
    factor_of = 1.0
    for dim, blocks in split:
        draws = jax.random.uniform(jax.random.fold_in(jax.random.fold_in(stream_key, 6), dim), (blocks,), jnp.float32, least / len(split), high / len(split))
        factor_of = factor_of * jnp.repeat(jnp.exp(draws), shape[dim] // blocks).reshape((-1,) + (1,) * (len(shape) - 1 - dim))
    return factor_of


def scatter_about(stream_key, shape, scale, most, split=(), kind=jnp.bfloat16):
    result = jax.random.normal(stream_key, shape, jnp.float32) * scale
    if len(split) > 0:
        result = level_of(stream_key, shape, split, -0.22, 0.18) * result
    return jnp.clip(result, min=-most, max=most).astype(kind)


def setup_inputs(seed: int = 0) -> dict:
    streams_of = jax.random.split(jax.random.key(seed), 18)
    return {
        "tokens": scatter_about(streams_of[0], (TOKENS, D), 1.0, 6.0, ((0, 8), (1, 4))),
        "norm1_gain": jnp.clip(1.0 + 0.15 * jax.random.normal(streams_of[1], (D,), jnp.float32), 0.25, 1.75),
        "norm1_bias": scatter_about(streams_of[2], (D,), 0.5, 3.0, (), jnp.float32),
        "qkv_weight": scatter_about(streams_of[3], (D, 3 * D), D ** -0.5, 0.1875, ((1, 4),)),
        "query_bias": scatter_about(streams_of[4], (D,), 0.5, 3.0, ((0, 4),), jnp.float32),
        "value_bias": scatter_about(streams_of[5], (D,), 0.5, 3.0, ((0, 4),), jnp.float32),
        "out_weight": scatter_about(streams_of[6], (D, D), (HD // 4) ** -0.5, 1.5, ((0, 4),)),
        "out_bias": scatter_about(streams_of[7], (D,), 0.3, 2.0, (), jnp.float32),
        "layer_scale1": jnp.clip(jnp.exp(jax.random.uniform(streams_of[8], (D,), jnp.float32, math.log(0.25), math.log(2.5))), 0.25, 2.5),
        "norm2_gain": jnp.clip(1.0 + 0.15 * jax.random.normal(streams_of[9], (D,), jnp.float32), 0.25, 1.75),
        "norm2_bias": scatter_about(streams_of[10], (D,), 0.5, 3.0, (), jnp.float32),
        "up_weight": scatter_about(streams_of[11], (D, FF), D ** -0.5, 0.1875, ((1, 4),)),
        "up_bias": scatter_about(streams_of[12], (FF,), 0.5, 3.0, ((0, 4),), jnp.float32),
        "down_weight": scatter_about(streams_of[13], (FF, D), FF ** -0.5, 0.09375, ((0, 4),)),
        "down_bias": scatter_about(streams_of[14], (D,), 0.3, 2.0, ((0, 4),), jnp.float32),
        "layer_scale2": jnp.clip(jnp.exp(math.log(2.5) - 2.3025851 * jax.random.uniform(streams_of[15], (D,), jnp.float32) ** level_of(streams_of[15], (D,), ((0, 4),), -0.2, 0.2)), 0.25, 2.5),
        "cotangent": scatter_about(streams_of[16], (TOKENS, D), 1.0, 6.0, ((0, 8), (1, 4))),
    }


EPS = 1e-06

def layer_norm(values, gain, bias):
    row_mean = lax.optimization_barrier(jnp.mean(values, axis=-1, keepdims=True))
    centred = values - row_mean
    inv_std = lax.rsqrt(lax.optimization_barrier(jnp.mean(centred * centred, axis=-1, keepdims=True)) + EPS)
    normed = centred * inv_std
    return (normed, inv_std, normed * gain + bias)

def norm_back(upstream, normed, inv_std, gain):
    scaled = upstream * gain
    return inv_std * (scaled - lax.optimization_barrier(jnp.mean(scaled, axis=-1, keepdims=True)) - normed * lax.optimization_barrier(jnp.mean(scaled * normed, axis=-1, keepdims=True)))

def gelu_parts(hidden_pre):
    cdf_value = 0.5 * (1.0 + jax.scipy.special.erf(hidden_pre * 2.0 ** (-0.5)))
    density = jnp.exp(-0.5 * hidden_pre * hidden_pre) * (2.0 * math.pi) ** (-0.5)
    return (hidden_pre * cdf_value, cdf_value + hidden_pre * density)

def lowered(values):
    return lax.optimization_barrier(values.astype(jnp.bfloat16)).astype(jnp.float32)

def group_sum(left, right, groups):
    width = left.shape[1] // groups
    total = jnp.zeros((left.shape[0], right.shape[1]), jnp.float32)
    for group in range(groups):
        part = jnp.dot(left[:, group * width:(group + 1) * width], right[group * width:(group + 1) * width], preferred_element_type=jnp.float32)
        total = total + lowered(part)
    return total

def attend(packed):
    query_rows, key_rows, value_rows = packed
    factor = query_rows.shape[-1] ** (-0.5)
    scores = jnp.einsum('qhd,khd->hqk', query_rows.astype(jnp.float32), key_rows.astype(jnp.float32)) * factor
    log_total = jax.nn.logsumexp(scores, axis=-1)
    probs = jnp.exp(scores - log_total[..., None])
    mixed = jnp.einsum('hqk,khd->qhd', lowered(probs), value_rows.astype(jnp.float32))
    return (mixed.astype(jnp.bfloat16), log_total)

def attend_back(packed):
    query_rows, key_rows, value_rows, log_total, grad_mixed = packed
    factor = query_rows.shape[-1] ** (-0.5)
    query_f = query_rows.astype(jnp.float32)
    key_f = key_rows.astype(jnp.float32)
    value_f = value_rows.astype(jnp.float32)
    grad_f = grad_mixed.astype(jnp.float32)
    scores = jnp.einsum('qhd,khd->hqk', query_f, key_f) * factor
    probs = jnp.exp(scores - log_total[..., None])
    grad_value = jnp.einsum('hqk,qhd->khd', lowered(probs), grad_f)
    grad_probs = jnp.einsum('qhd,khd->hqk', grad_f, value_f)
    delta = lax.optimization_barrier(jnp.sum(probs * grad_probs, axis=-1, keepdims=True))
    grad_scores = lowered(probs * (grad_probs - delta) * factor)
    grad_query = jnp.einsum('hqk,khd->qhd', grad_scores, key_f)
    grad_key = jnp.einsum('hqk,qhd->khd', grad_scores, query_f)
    return (grad_query, grad_key, grad_value)

def reference(tokens, norm1_gain, norm1_bias, qkv_weight, query_bias, value_bias, out_weight, out_bias, layer_scale1, norm2_gain, norm2_bias, up_weight, up_bias, down_weight, down_bias, layer_scale2, cotangent):
    row_count = tokens.shape[0]
    images = row_count // TOK_IMG
    whole = tokens.astype(jnp.float32)
    normed1, inv_std1, scaled1 = layer_norm(whole, norm1_gain, norm1_bias)
    lowered1 = scaled1.astype(jnp.bfloat16)
    projected = jnp.dot(lowered1, qkv_weight, preferred_element_type=jnp.float32).reshape(row_count, H, 3, HD)
    query_rows = (projected[:, :, 0] + query_bias.reshape(H, HD)).astype(jnp.bfloat16).reshape(images, TOK_IMG, H, HD)
    key_rows = projected[:, :, 1].astype(jnp.bfloat16).reshape(images, TOK_IMG, H, HD)
    value_rows = (projected[:, :, 2] + value_bias.reshape(H, HD)).astype(jnp.bfloat16).reshape(images, TOK_IMG, H, HD)
    mixed, log_total = lax.map(attend, (query_rows, key_rows, value_rows))
    mixed_flat = mixed.reshape(row_count, D)
    attended = group_sum(mixed_flat, out_weight, N_TENSOR) + out_bias
    residual = whole + layer_scale1 * attended
    normed2, inv_std2, scaled2 = layer_norm(residual, norm2_gain, norm2_bias)
    lowered2 = scaled2.astype(jnp.bfloat16)
    hidden_pre = jnp.dot(lowered2, up_weight, preferred_element_type=jnp.float32) + up_bias
    activated, slope = gelu_parts(hidden_pre)
    activated_low = activated.astype(jnp.bfloat16)
    branch = group_sum(activated_low, down_weight, N_TENSOR) + down_bias
    output = residual + layer_scale2 * branch
    upstream = cotangent.astype(jnp.float32)
    grad_layer_scale2 = lax.optimization_barrier(jnp.sum(upstream * branch, axis=0))
    grad_down_bias = lax.optimization_barrier(jnp.sum(upstream * layer_scale2, axis=0))
    branch_grad = (upstream * layer_scale2).astype(jnp.bfloat16)
    grad_down_weight = jnp.dot(activated_low.T, branch_grad, preferred_element_type=jnp.float32)
    grad_hidden = jnp.dot(branch_grad, down_weight.T, preferred_element_type=jnp.float32)
    grad_pre = grad_hidden * slope
    grad_up_bias = lax.optimization_barrier(jnp.sum(grad_pre, axis=0))
    grad_pre_low = grad_pre.astype(jnp.bfloat16)
    grad_up_weight = jnp.dot(lowered2.T, grad_pre_low, preferred_element_type=jnp.float32)
    grad_lowered2 = group_sum(grad_pre_low, up_weight.T, N_TENSOR)
    grad_norm2_gain = lax.optimization_barrier(jnp.sum(grad_lowered2 * normed2, axis=0))
    grad_norm2_bias = lax.optimization_barrier(jnp.sum(grad_lowered2, axis=0))
    grad_residual = upstream + norm_back(grad_lowered2, normed2, inv_std2, norm2_gain)
    grad_layer_scale1 = lax.optimization_barrier(jnp.sum(grad_residual * attended, axis=0))
    grad_out_bias = lax.optimization_barrier(jnp.sum(grad_residual * layer_scale1, axis=0))
    grad_attended = (grad_residual * layer_scale1).astype(jnp.bfloat16)
    grad_out_weight = jnp.dot(mixed_flat.T, grad_attended, preferred_element_type=jnp.float32)
    grad_mixed = jnp.dot(grad_attended, out_weight.T, preferred_element_type=jnp.float32).astype(jnp.bfloat16)
    grad_mixed = grad_mixed.reshape(images, TOK_IMG, H, HD)
    grad_query, grad_key, grad_value = lax.map(attend_back, (query_rows, key_rows, value_rows, log_total, grad_mixed))
    grad_query_bias = lax.optimization_barrier(jnp.sum(grad_query, axis=(0, 1))).reshape(D)
    grad_value_bias = lax.optimization_barrier(jnp.sum(grad_value, axis=(0, 1))).reshape(D)
    grad_projected = jnp.stack([grad_query, grad_key, grad_value], axis=3).reshape(row_count, 3 * D).astype(jnp.bfloat16)
    grad_qkv_weight = jnp.dot(lowered1.T, grad_projected, preferred_element_type=jnp.float32)
    grad_lowered1 = group_sum(grad_projected, qkv_weight.T, N_TENSOR)
    grad_norm1_gain = lax.optimization_barrier(jnp.sum(grad_lowered1 * normed1, axis=0))
    grad_norm1_bias = lax.optimization_barrier(jnp.sum(grad_lowered1, axis=0))
    input_grad = grad_residual + norm_back(grad_lowered1, normed1, inv_std1, norm1_gain)
    return (output, input_grad, grad_norm1_gain, grad_norm1_bias, grad_qkv_weight, grad_query_bias, grad_value_bias, grad_out_weight, grad_out_bias, grad_layer_scale1, grad_norm2_gain, grad_norm2_bias, grad_up_weight, grad_up_bias, grad_down_weight, grad_down_bias, grad_layer_scale2)
```

```python
import math

import jax
import jax.numpy as jnp
from jax import lax
from jax.sharding import PartitionSpec as P

HD = 64
TOK_IMG = 257


EPS = 1e-06


def layer_norm(values, gain, bias):
    row_mean = jnp.mean(values, axis=-1, keepdims=True)
    centred = values - row_mean
    inv_std = lax.rsqrt(jnp.mean(centred * centred, axis=-1, keepdims=True) + EPS)
    normed = centred * inv_std
    return (normed, inv_std, normed * gain + bias)


def norm_back(upstream, normed, inv_std, gain):
    scaled = upstream * gain
    return inv_std * (
        scaled
        - jnp.mean(scaled, axis=-1, keepdims=True)
        - normed * jnp.mean(scaled * normed, axis=-1, keepdims=True)
    )


def gelu_parts(hidden_pre):
    cdf_value = 0.5 * (1.0 + jax.scipy.special.erf(hidden_pre * 2.0 ** (-0.5)))
    density = jnp.exp(-0.5 * hidden_pre * hidden_pre) * (2.0 * math.pi) ** (-0.5)
    return (hidden_pre * cdf_value, cdf_value + hidden_pre * density)


def contract_rows(left, right):
    return lax.dot_general(
        left, right, (((0,), (0,)), ((), ())), preferred_element_type=jnp.float32
    )


def contract_cols(left, right):
    return lax.dot_general(
        left, right, (((1,), (1,)), ((), ())), preferred_element_type=jnp.float32
    )


def score_probs(query_rows, key_rows, log_total):
    scores = jnp.einsum(
        "iqhd,ikhd->ihqk", query_rows, key_rows, preferred_element_type=jnp.float32
    ) * HD ** (-0.5)
    return jnp.exp(scores - log_total[..., None])


def exchange(block, axis, bit):
    size = lax.axis_size(axis)
    return lax.ppermute(block, axis, [(index, index ^ (1 << bit)) for index in range(size)])


def bit_of(axis, bit):
    return (lax.axis_index(axis) >> bit) % 2 == 1


def bits_in(axis):
    return (lax.axis_size(axis) - 1).bit_length()


def gather_cols(block, axis):
    width = block.shape[-1]
    for bit in range(1, bits_in(axis)):
        got = exchange(block, axis, bit)
        upper = bit_of(axis, bit)
        block = jnp.concatenate(
            [jnp.where(upper, got, block), jnp.where(upper, block, got)], axis=-1
        )
    got = exchange(block, axis, 0)
    upper = bit_of(axis, 0)
    pieces = []
    for start in range(0, block.shape[-1], width):
        mine, theirs = (part[..., start : start + width] for part in (block, got))
        pieces += [jnp.where(upper, theirs, mine), jnp.where(upper, mine, theirs)]
    return jnp.concatenate(pieces, axis=-1)


def sum_all(part, axis):
    half = part.shape[-1] // 2
    upper = bit_of(axis, 0)
    low, high = part[..., :half], part[..., half:]
    got = exchange(jnp.where(upper, low, high), axis, 0)
    total = jnp.where(upper, high, low).astype(jnp.float32) + got.astype(jnp.float32)
    for bit in range(1, bits_in(axis)):
        sent = total.astype(jnp.bfloat16)
        got = exchange(sent, axis, bit)
        total = sent.astype(jnp.float32) + got.astype(jnp.float32)
    sent = total.astype(jnp.bfloat16)
    got = exchange(sent, axis, 0)
    return jnp.concatenate([jnp.where(upper, got, sent), jnp.where(upper, sent, got)], axis=-1)


def sum_scatter_cols(part, axis):
    count = lax.axis_size(axis)
    width = part.shape[-1] // count
    upper = bit_of(axis, 0)
    blocks = [part[..., index * width : (index + 1) * width] for index in range(count)]
    even = jnp.concatenate(blocks[0::2], axis=-1)
    odd = jnp.concatenate(blocks[1::2], axis=-1)
    got = exchange(jnp.where(upper, even, odd), axis, 0)
    total = jnp.where(upper, odd, even).astype(jnp.float32) + got.astype(jnp.float32)
    for bit in reversed(range(1, bits_in(axis))):
        half = total.shape[-1] // 2
        upper = bit_of(axis, bit)
        low, high = total[..., :half], total[..., half:]
        got = exchange(jnp.where(upper, low, high).astype(jnp.bfloat16), axis, bit)
        total = jnp.where(upper, high, low) + got.astype(jnp.float32)
    return total


def sum_rows(grad, axis, order):
    for bit in order:
        half = grad.shape[0] // 2
        upper = bit_of(axis, bit)
        low, high = grad[:half], grad[half:]
        got = exchange(jnp.where(upper, low, high).astype(jnp.bfloat16), axis, bit)
        grad = jnp.where(upper, high, low) + got.astype(jnp.float32)
    grad = grad.astype(jnp.bfloat16)
    for bit in reversed(order):
        got = exchange(grad, axis, bit)
        upper = bit_of(axis, bit)
        grad = jnp.concatenate([jnp.where(upper, got, grad), jnp.where(upper, grad, got)], axis=0)
    return grad.astype(jnp.float32)


def sum_small(values, axis):
    packed = jnp.concatenate(values)
    for bit in range(bits_in(axis)):
        packed = packed + exchange(packed, axis, bit)
    result, start = [], 0
    for value in values:
        result.append(packed[start : start + value.shape[0]])
        start += value.shape[0]
    return result


def shards(
    tokens,
    norm1_gain,
    norm1_bias,
    qkv_weight,
    query_bias,
    value_bias,
    out_weight,
    out_bias,
    layer_scale1,
    norm2_gain,
    norm2_bias,
    up_weight,
    up_bias,
    down_weight,
    down_bias,
    layer_scale2,
    cotangent,
):
    whole = gather_cols(tokens, "tensor").astype(jnp.float32)
    upstream = gather_cols(cotangent, "tensor").astype(jnp.float32)
    scale2_all = lax.all_gather(layer_scale2, "tensor", axis=0, tiled=True)
    row_count = whole.shape[0]
    images = row_count // TOK_IMG
    heads_local = qkv_weight.shape[1] // (3 * HD)
    shape_heads = (images, TOK_IMG, heads_local, HD)
    normed1, inv_std1, scaled1 = layer_norm(whole, norm1_gain, norm1_bias)
    lowered1 = scaled1.astype(jnp.bfloat16)
    projected = jnp.dot(lowered1, qkv_weight, preferred_element_type=jnp.float32).reshape(
        row_count, heads_local, 3, HD
    )
    query_rows = (
        (projected[:, :, 0] + query_bias.reshape(heads_local, HD))
        .astype(jnp.bfloat16)
        .reshape(shape_heads)
    )
    key_rows = projected[:, :, 1].astype(jnp.bfloat16).reshape(shape_heads)
    value_rows = (
        (projected[:, :, 2] + value_bias.reshape(heads_local, HD))
        .astype(jnp.bfloat16)
        .reshape(shape_heads)
    )
    scores = jnp.einsum(
        "iqhd,ikhd->ihqk", query_rows, key_rows, preferred_element_type=jnp.float32
    ) * HD ** (-0.5)
    log_total = jax.nn.logsumexp(scores, axis=-1)
    probs = jnp.exp(scores - log_total[..., None])
    mixed = (
        jnp.einsum(
            "ihqk,ikhd->iqhd",
            probs.astype(jnp.bfloat16),
            value_rows,
            preferred_element_type=jnp.float32,
        )
        .astype(jnp.bfloat16)
        .reshape(row_count, heads_local * HD)
    )
    attention_part = jnp.dot(mixed, out_weight, preferred_element_type=jnp.float32)
    attended = sum_all(attention_part.astype(jnp.bfloat16), "tensor").astype(jnp.float32) + out_bias
    residual = whole + layer_scale1 * attended
    normed2, inv_std2, scaled2 = layer_norm(residual, norm2_gain, norm2_bias)
    lowered2 = scaled2.astype(jnp.bfloat16)
    hidden_pre = jnp.dot(lowered2, up_weight, preferred_element_type=jnp.float32) + up_bias
    activated, slope = gelu_parts(hidden_pre)
    activated_low = activated.astype(jnp.bfloat16)
    down_part = jnp.dot(activated_low, down_weight, preferred_element_type=jnp.float32)
    branch_cols = sum_scatter_cols(down_part.astype(jnp.bfloat16), "tensor") + down_bias
    width_local = tokens.shape[1]
    col_start = lax.axis_index("tensor") * width_local
    residual_cols = lax.dynamic_slice_in_dim(residual, col_start, width_local, 1)
    output = residual_cols + layer_scale2 * branch_cols
    upstream_cols = cotangent.astype(jnp.float32)
    grad_layer_scale2 = jnp.sum(upstream_cols * branch_cols, axis=0)
    grad_down_bias = jnp.sum(upstream_cols * layer_scale2, axis=0)
    branch_grad = (upstream * scale2_all).astype(jnp.bfloat16)
    grad_down_weight = contract_rows(activated_low, branch_grad)
    grad_hidden = contract_cols(branch_grad, down_weight)
    grad_pre = grad_hidden * slope
    grad_up_bias = jnp.sum(grad_pre, axis=0)
    grad_pre_low = grad_pre.astype(jnp.bfloat16)
    grad_up_weight = contract_rows(lowered2, grad_pre_low)
    grad_lowered2 = sum_all(
        contract_cols(grad_pre_low, up_weight).astype(jnp.bfloat16), "tensor"
    ).astype(jnp.float32)
    grad_norm2_gain = jnp.sum(grad_lowered2 * normed2, axis=0)
    grad_norm2_bias = jnp.sum(grad_lowered2, axis=0)
    grad_residual = upstream + norm_back(grad_lowered2, normed2, inv_std2, norm2_gain)
    grad_layer_scale1 = jnp.sum(grad_residual * attended, axis=0)
    grad_out_bias = jnp.sum(grad_residual * layer_scale1, axis=0)
    grad_attended = (grad_residual * layer_scale1).astype(jnp.bfloat16)
    grad_out_weight = contract_rows(mixed, grad_attended)
    grad_mixed = contract_cols(grad_attended, out_weight).astype(jnp.bfloat16).reshape(shape_heads)
    probs_back = score_probs(query_rows, key_rows, log_total)
    grad_value = jnp.einsum(
        "ihqk,iqhd->ikhd",
        probs_back.astype(jnp.bfloat16),
        grad_mixed,
        preferred_element_type=jnp.float32,
    )
    grad_probs = jnp.einsum(
        "iqhd,ikhd->ihqk", grad_mixed, value_rows, preferred_element_type=jnp.float32
    )
    delta = jnp.sum(probs_back * grad_probs, axis=-1, keepdims=True)
    grad_scores = (probs_back * (grad_probs - delta) * HD ** (-0.5)).astype(jnp.bfloat16)
    grad_query = jnp.einsum(
        "ihqk,ikhd->iqhd", grad_scores, key_rows, preferred_element_type=jnp.float32
    )
    grad_key = jnp.einsum(
        "ihqk,iqhd->ikhd", grad_scores, query_rows, preferred_element_type=jnp.float32
    )
    grad_query_bias = jnp.sum(grad_query, axis=(0, 1)).reshape(heads_local * HD)
    grad_value_bias = jnp.sum(grad_value, axis=(0, 1)).reshape(heads_local * HD)
    grad_projected = (
        jnp.stack([grad_query, grad_key, grad_value], axis=3)
        .reshape(row_count, 3 * heads_local * HD)
        .astype(jnp.bfloat16)
    )
    grad_qkv_weight = contract_rows(lowered1, grad_projected)
    def cols(values):
        return lax.dynamic_slice_in_dim(values, col_start, width_local, values.ndim - 1)

    grad_lowered1 = sum_scatter_cols(
        contract_cols(grad_projected, qkv_weight).astype(jnp.bfloat16), "tensor"
    )
    normed1_cols = cols(normed1)
    features = whole.shape[1]
    scaled = grad_lowered1 * cols(norm1_gain)
    row_sums = sum_small(
        [jnp.sum(scaled, axis=-1), jnp.sum(scaled * normed1_cols, axis=-1)], "tensor"
    )
    mean_scaled, mean_product = (values[:, None] / features for values in row_sums)
    input_grad = cols(grad_residual) + inv_std1 * (
        scaled - mean_scaled - normed1_cols * mean_product
    )
    order = tuple(range(bits_in("dp")))
    swapped = order[1:2] + order[:1] + order[2:]
    grad_down_weight = sum_rows(grad_down_weight, "dp", order)
    grad_up_weight = sum_rows(grad_up_weight, "dp", swapped)
    grad_out_weight = sum_rows(grad_out_weight, "dp", order)
    middle = grad_qkv_weight.shape[0] // 2
    grad_qkv_weight = jnp.concatenate(
        [
            sum_rows(grad_qkv_weight[:middle], "dp", order),
            sum_rows(grad_qkv_weight[middle:], "dp", swapped),
        ],
        axis=0,
    )
    (
        grad_query_bias,
        grad_value_bias,
        grad_out_bias,
        grad_layer_scale1,
        grad_norm2_gain,
        grad_norm2_bias,
        grad_up_bias,
        grad_down_bias,
        grad_layer_scale2,
    ) = sum_small(
        [
            grad_query_bias,
            grad_value_bias,
            grad_out_bias,
            grad_layer_scale1,
            grad_norm2_gain,
            grad_norm2_bias,
            grad_up_bias,
            grad_down_bias,
            grad_layer_scale2,
        ],
        "dp",
    )
    norm1_sums = jnp.stack(
        sum_small(
            [jnp.sum(grad_lowered1 * normed1_cols, axis=0), jnp.sum(grad_lowered1, axis=0)], "dp"
        )
    )
    grad_norm1_gain, grad_norm1_bias = gather_cols(norm1_sums, "tensor")
    return (
        output,
        input_grad,
        grad_norm1_gain,
        grad_norm1_bias,
        grad_qkv_weight,
        grad_query_bias,
        grad_value_bias,
        grad_out_weight,
        grad_out_bias,
        grad_layer_scale1,
        grad_norm2_gain,
        grad_norm2_bias,
        grad_up_weight,
        grad_up_bias,
        grad_down_weight,
        grad_down_bias,
        grad_layer_scale2,
    )


def solution(mesh):
    return jax.shard_map(
        shards,
        mesh=mesh,
        in_specs=(
            P("dp", "tensor"),
            P(),
            P(),
            P(None, "tensor"),
            P("tensor"),
            P("tensor"),
            P("tensor", None),
            P(),
            P(),
            P(),
            P(),
            P(None, "tensor"),
            P("tensor"),
            P("tensor", None),
            P("tensor"),
            P("tensor"),
            P("dp", "tensor"),
        ),
        out_specs=(
            P("dp", "tensor"),
            P("dp", "tensor"),
            P(),
            P(),
            P(None, "tensor"),
            P("tensor"),
            P("tensor"),
            P("tensor", None),
            P(),
            P(),
            P(),
            P(),
            P(None, "tensor"),
            P("tensor"),
            P("tensor", None),
            P("tensor"),
            P("tensor"),
        ),
        check_vma=False,
    )
```

```python
import math

import jax
import jax.numpy as jnp
from jax import lax
from jax.experimental import pallas as pl
from jax.experimental.pallas import tpu as pltpu
from jax.sharding import PartitionSpec as P

HD = 64
TOK_IMG = 257


EPS = 1e-06


def layer_norm(values, gain, bias):
    row_mean = jnp.mean(values, axis=-1, keepdims=True)
    centred = values - row_mean
    inv_std = lax.rsqrt(jnp.mean(centred * centred, axis=-1, keepdims=True) + EPS)
    normed = centred * inv_std
    return (normed, inv_std, normed * gain + bias)


def norm_back(upstream, normed, inv_std, gain):
    scaled = upstream * gain
    return inv_std * (
        scaled
        - jnp.mean(scaled, axis=-1, keepdims=True)
        - normed * jnp.mean(scaled * normed, axis=-1, keepdims=True)
    )


def gelu_parts(hidden_pre):
    cdf_value = 0.5 * (1.0 + jax.scipy.special.erf(hidden_pre * 2.0 ** (-0.5)))
    density = jnp.exp(-0.5 * hidden_pre * hidden_pre) * (2.0 * math.pi) ** (-0.5)
    return (hidden_pre * cdf_value, cdf_value + hidden_pre * density)


def contract_rows(left, right):
    return lax.dot_general(
        left, right, (((0,), (0,)), ((), ())), preferred_element_type=jnp.float32
    )


def contract_cols(left, right):
    return lax.dot_general(
        left, right, (((1,), (1,)), ((), ())), preferred_element_type=jnp.float32
    )


HEAD_COLS = 3 * HD


def probs_of(packed, head, keep):
    start = head * HEAD_COLS
    query = packed[:, start : start + HD]
    key = packed[:, start + HD : start + 2 * HD]
    value = packed[:, start + 2 * HD : start + 3 * HD]
    scores = jnp.where(keep, contract_cols(key, query) * HD ** (-0.5), -1e30)
    powers = jnp.exp(scores - jnp.max(scores, axis=0, keepdims=True))
    probs = powers * (1.0 / jnp.sum(powers, axis=0, keepdims=True))
    return query, key, value, probs


def forward_kernel(
    tokens, gain, bias, weight, proj_bias, out_mine, out_theirs, low, packed, mixed, mine, theirs
):
    rows = tokens.shape[1]
    _, _, scaled = layer_norm(tokens[0].astype(jnp.float32), gain[...], bias[...])
    low[0] = scaled.astype(jnp.bfloat16)
    projected = jnp.dot(low[0], weight[...], preferred_element_type=jnp.float32)
    packed[0] = (projected + proj_bias[...]).astype(jnp.bfloat16)
    keep = lax.broadcasted_iota(jnp.int32, (rows, rows), 0) < TOK_IMG
    columns = packed[0]
    outs = []
    for head in range(weight.shape[1] // HEAD_COLS):
        _, _, value, probs = probs_of(columns, head, keep)
        outs.append(
            jnp.dot(
                value.astype(jnp.float32).T.astype(jnp.bfloat16),
                probs.astype(jnp.bfloat16),
                preferred_element_type=jnp.float32,
            )
        )
    mixed[0] = jnp.concatenate(outs, axis=0).T.astype(jnp.bfloat16)
    for part, out_weight in ((mine, out_mine), (theirs, out_theirs)):
        part[0] = jnp.dot(
            mixed[0], out_weight[...], preferred_element_type=jnp.float32
        ).astype(jnp.bfloat16)


def backward_kernel(
    packed, upstream, out_weight, back_mine, back_theirs, grad, mine, theirs, query_sum, value_sum
):
    rows = packed.shape[1]
    heads = packed.shape[2] // HEAD_COLS

    @pl.when(pl.program_id(0) == 0)
    def _():
        query_sum[...] = jnp.zeros_like(query_sum)
        value_sum[...] = jnp.zeros_like(value_sum)

    grad_mixed = contract_cols(upstream[0], out_weight[...]).astype(jnp.bfloat16)
    keep = lax.broadcasted_iota(jnp.int32, (rows, rows), 0) < TOK_IMG
    columns = packed[0]
    queries = []
    for head in range(heads):
        query, key, value, probs = probs_of(columns, head, keep)
        grad_head = grad_mixed[:, head * HD : (head + 1) * HD]
        grad_probs = contract_cols(value, grad_head)
        delta = jnp.sum(probs * grad_probs, axis=0, keepdims=True)
        grad_scores = (probs * (grad_probs - delta) * HD ** (-0.5)).astype(jnp.bfloat16)
        grad_value = jnp.dot(
            probs.astype(jnp.bfloat16), grad_head, preferred_element_type=jnp.float32
        )
        grad_key = jnp.dot(grad_scores, query, preferred_element_type=jnp.float32)
        queries.append(
            jnp.dot(
                key.astype(jnp.float32).T.astype(jnp.bfloat16),
                grad_scores,
                preferred_element_type=jnp.float32,
            )
        )
        start = head * HEAD_COLS
        grad[0, :, start + HD : start + 2 * HD] = grad_key.astype(jnp.bfloat16)
        grad[0, :, start + 2 * HD : start + 3 * HD] = grad_value.astype(jnp.bfloat16)
        value_sum[:, head * HD : (head + 1) * HD] += jnp.sum(grad_value, axis=0, keepdims=True)
    grad_query = jnp.concatenate(queries, axis=0).T
    query_sum[...] += jnp.sum(grad_query, axis=0, keepdims=True)
    for head in range(heads):
        start = head * HEAD_COLS
        grad[0, :, start : start + HD] = grad_query[:, head * HD : (head + 1) * HD].astype(
            jnp.bfloat16
        )
    for part, weight in ((mine, back_mine), (theirs, back_theirs)):
        part[0] = contract_cols(grad[0], weight[...]).astype(jnp.bfloat16)


def per_image(shape):
    return pl.BlockSpec((1,) + shape[1:], lambda image: (image, 0, 0))


def resident(shape):
    return pl.BlockSpec(shape, lambda image: (0, 0))


def run_images(kernel, images, args, outs, name):
    spec = lambda shape: per_image(shape) if len(shape) == 3 else resident(shape)
    return pl.pallas_call(
        kernel,
        grid=(images,),
        in_specs=[spec(arg.shape) for arg in args],
        out_specs=[spec(out.shape) for out in outs],
        out_shape=outs,
        compiler_params=pltpu.CompilerParams(vmem_limit_bytes=48 << 20),
        name=name,
    )(*args)


def attention_forward(tokens, gain, bias, weight, proj_bias, out_mine, out_theirs):
    images, rows, features = tokens.shape
    struct = lambda width: jax.ShapeDtypeStruct((images, rows, width), jnp.bfloat16)
    half = out_mine.shape[1]
    outs = [
        struct(features),
        struct(weight.shape[1]),
        struct(out_mine.shape[0]),
        struct(half),
        struct(half),
    ]
    args = (tokens, gain, bias, weight, proj_bias, out_mine, out_theirs)
    return run_images(forward_kernel, images, args, outs, "attention_forward")


def attention_backward(packed, upstream, out_weight, back_mine, back_theirs):
    images, rows, width = packed.shape
    struct = lambda columns: jax.ShapeDtypeStruct((images, rows, columns), jnp.bfloat16)
    sums = jax.ShapeDtypeStruct((1, width // 3), jnp.float32)
    half = back_mine.shape[0]
    outs = [struct(width), struct(half), struct(half), sums, sums]
    args = (packed, upstream, out_weight, back_mine, back_theirs)
    return run_images(backward_kernel, images, args, outs, "attention_backward")


def exchange(block, axis, bit):
    size = lax.axis_size(axis)
    return lax.ppermute(block, axis, [(index, index ^ (1 << bit)) for index in range(size)])


def bit_of(axis, bit):
    return (lax.axis_index(axis) >> bit) % 2 == 1


def bits_in(axis):
    return (lax.axis_size(axis) - 1).bit_length()


def after(value, *others):
    return lax.optimization_barrier((value, *others))[0]


def split_blocks(values, dim):
    count = lax.axis_size("tensor")
    blocks = jnp.split(values, count, axis=dim)
    even = jnp.concatenate(blocks[0::2], axis=dim)
    odd = jnp.concatenate(blocks[1::2], axis=dim)
    upper = bit_of("tensor", 0)
    return jnp.where(upper, odd, even), jnp.where(upper, even, odd)


def join_blocks(mine, theirs):
    count = lax.axis_size("tensor") // 2
    upper = bit_of("tensor", 0)
    pieces = []
    for own, other in zip(jnp.split(mine, count, axis=-1), jnp.split(theirs, count, axis=-1)):
        pieces += [jnp.where(upper, other, own), jnp.where(upper, own, other)]
    return jnp.concatenate(pieces, axis=-1)


def gather_far(block):
    for bit in range(1, bits_in("tensor")):
        got = exchange(block, "tensor", bit)
        upper = bit_of("tensor", bit)
        block = jnp.concatenate(
            [jnp.where(upper, got, block), jnp.where(upper, block, got)], axis=-1
        )
    return block


def gather_near(block):
    return join_blocks(block, exchange(block, "tensor", 0))


def add_near(mine, theirs):
    return mine.astype(jnp.float32) + exchange(theirs, "tensor", 0).astype(jnp.float32)


def add_far(total):
    for bit in range(1, bits_in("tensor")):
        sent = total.astype(jnp.bfloat16)
        total = sent.astype(jnp.float32) + exchange(sent, "tensor", bit).astype(jnp.float32)
    return total.astype(jnp.bfloat16)


def scatter_far(total):
    for bit in reversed(range(1, bits_in("tensor"))):
        low, high = jnp.split(total, 2, axis=-1)
        upper = bit_of("tensor", bit)
        got = exchange(jnp.where(upper, low, high).astype(jnp.bfloat16), "tensor", bit)
        total = jnp.where(upper, high, low) + got.astype(jnp.float32)
    return total


def halve_rows(grad, bit):
    low, high = jnp.split(grad, 2, axis=0)
    upper = bit_of("dp", bit)
    got = exchange(jnp.where(upper, low, high).astype(jnp.bfloat16), "dp", bit)
    return jnp.where(upper, high, low) + got.astype(jnp.float32)


def double_rows(grad, bit):
    got = exchange(grad, "dp", bit)
    upper = bit_of("dp", bit)
    return jnp.concatenate([jnp.where(upper, got, grad), jnp.where(upper, grad, got)], axis=0)


def sum_rows(grad, order):
    for bit in order:
        grad = halve_rows(grad, bit)
    grad = grad.astype(jnp.bfloat16)
    for bit in reversed(order):
        grad = double_rows(grad, bit)
    return grad.astype(jnp.float32)


def sum_small(values, axis):
    packed = jnp.concatenate(values)
    for bit in range(bits_in(axis)):
        packed = packed + exchange(packed, axis, bit)
    result, start = [], 0
    for value in values:
        result.append(packed[start : start + value.shape[0]])
        start += value.shape[0]
    return result


def shards(
    tokens,
    norm1_gain,
    norm1_bias,
    qkv_weight,
    query_bias,
    value_bias,
    out_weight,
    out_bias,
    layer_scale1,
    norm2_gain,
    norm2_bias,
    up_weight,
    up_bias,
    down_weight,
    down_bias,
    layer_scale2,
    cotangent,
):
    images = tokens.shape[0] // TOK_IMG
    width_local = tokens.shape[1]
    features = norm1_gain.shape[0]
    padded = -(-TOK_IMG // 8) * 8
    heads_local = query_bias.shape[0] // HD
    chunks = 2 if images % 2 == 0 else 1
    col_start = lax.axis_index("tensor") * width_local
    order = tuple(range(bits_in("dp")))
    swapped = order[1:2] + order[:1] + order[2:]

    def cols(values):
        return lax.dynamic_slice_in_dim(values, col_start, width_local, values.ndim - 1)

    def pad_rows(values):
        values = values.reshape(images, TOK_IMG, width_local)
        return jnp.pad(values, ((0, 0), (0, padded - TOK_IMG), (0, 0)))

    def flat(values):
        return values.reshape(-1, values.shape[-1])

    def unpad_rows(values):
        values = values.reshape(images, padded, width_local)
        return values[:, :TOK_IMG].reshape(images * TOK_IMG, width_local)

    def in_chunks(values):
        return jnp.split(values, chunks, axis=0)

    def out_of_chunks(values):
        return jnp.concatenate(values, axis=0)

    tokens = pad_rows(tokens)
    cotangent = pad_rows(cotangent)
    out_mine, out_theirs = split_blocks(out_weight, 1)
    qkv_mine, qkv_theirs = split_blocks(qkv_weight, 0)
    up_mine, up_theirs = split_blocks(up_weight, 0)
    down_mine, down_theirs = split_blocks(down_weight, 1)
    proj_bias = jnp.stack(
        [
            query_bias.reshape(heads_local, HD),
            jnp.zeros((heads_local, HD), jnp.float32),
            value_bias.reshape(heads_local, HD),
        ],
        axis=1,
    ).reshape(1, 3 * heads_local * HD)
    tokens_far = [gather_far(part) for part in in_chunks(tokens)]
    scale2_all = gather_near(gather_far(layer_scale2[None]))
    whole = [gather_near(part) for part in tokens_far]
    cotangent_far = gather_far(after(cotangent, *tokens_far))
    upstream_low = gather_near(cotangent_far)

    forward = [
        attention_forward(
            part, norm1_gain[None], norm1_bias[None], qkv_weight, proj_bias, out_mine, out_theirs
        )
        for part in whole
    ]
    upstream = [flat(part) for part in in_chunks(upstream_low)]
    branch_grad = [(part.astype(jnp.float32) * scale2_all).astype(jnp.bfloat16) for part in upstream]

    attended_low, normed2, inv_std2, lowered2, residual = [], [], [], [], []
    activated_low, grad_pre, grad_pre_low = [], [], []
    for index in range(chunks):
        _, _, _, mine, theirs = forward[index]
        total = add_far(add_near(flat(mine), flat(theirs)))
        joined = gather_near(total)
        attended_low.append(joined)
        attended = joined.astype(jnp.float32) + out_bias
        residual.append(flat(whole[index]).astype(jnp.float32) + layer_scale1 * attended)
        normed, inv_std, scaled = layer_norm(residual[index], norm2_gain, norm2_bias)
        normed2.append(normed)
        inv_std2.append(inv_std)
        lowered2.append(scaled.astype(jnp.bfloat16))
        hidden_pre = (
            jnp.dot(lowered2[index], up_weight, preferred_element_type=jnp.float32) + up_bias
        )
        activated, slope = gelu_parts(hidden_pre)
        activated_low.append(activated.astype(jnp.bfloat16))
        grad_pre.append(contract_cols(branch_grad[index], down_weight) * slope)
        grad_pre_low.append(grad_pre[index].astype(jnp.bfloat16))

    lowered2_all = out_of_chunks(lowered2)
    activated_all = out_of_chunks(activated_low)
    grad_pre_all = out_of_chunks(grad_pre_low)
    branch_grad_all = out_of_chunks(branch_grad)
    grad_down_weight = contract_rows(activated_all, branch_grad_all)
    grad_up_weight = contract_rows(lowered2_all, grad_pre_all)
    grad_up_bias = sum(jnp.sum(part, axis=0) for part in grad_pre)

    grad_residual, grad_attended, sums2 = [], [], []
    back = []
    for index in range(chunks):
        total = add_far(
            add_near(
                contract_cols(grad_pre_low[index], up_mine).astype(jnp.bfloat16),
                contract_cols(grad_pre_low[index], up_theirs).astype(jnp.bfloat16),
            )
        )
        grad_lowered2 = gather_near(total).astype(jnp.float32)
        part = upstream[index].astype(jnp.float32) + norm_back(
            grad_lowered2, normed2[index], inv_std2[index], norm2_gain
        )
        grad_residual.append(part)
        attended = attended_low[index].astype(jnp.float32) + out_bias
        sums2.append(
            (
                jnp.sum(grad_lowered2 * normed2[index], axis=0),
                jnp.sum(grad_lowered2, axis=0),
                jnp.sum(part * attended, axis=0),
                jnp.sum(part * layer_scale1, axis=0),
            )
        )
        grad_attended.append((part * layer_scale1).astype(jnp.bfloat16))
        packed = forward[index][1]
        back.append(
            attention_backward(
                packed,
                grad_attended[index].reshape(packed.shape[:2] + (features,)),
                out_weight,
                qkv_mine,
                qkv_theirs,
            )
        )
    grad_norm2_gain, grad_norm2_bias, grad_layer_scale1, grad_out_bias = (
        sum(parts) for parts in zip(*sums2)
    )
    grad_query_bias = sum(parts[3] for parts in back)[0]
    grad_value_bias = sum(parts[4] for parts in back)[0]
    grad_out_weight = contract_rows(
        flat(out_of_chunks([parts[2] for parts in forward])), out_of_chunks(grad_attended)
    )
    grad_qkv_weight = contract_rows(
        flat(out_of_chunks([parts[0] for parts in forward])),
        flat(out_of_chunks([parts[0] for parts in back])),
    )
    grad_lowered1 = out_of_chunks(
        [scatter_far(add_near(flat(parts[1]), flat(parts[2]))) for parts in back]
    )

    branch_cols = (
        scatter_far(
            add_near(
                jnp.dot(
                    activated_all, down_mine, preferred_element_type=jnp.float32
                ).astype(jnp.bfloat16),
                jnp.dot(
                    activated_all, down_theirs, preferred_element_type=jnp.float32
                ).astype(jnp.bfloat16),
            )
        )
        + down_bias
    )
    output = out_of_chunks([cols(part) for part in residual]) + layer_scale2 * branch_cols
    upstream_cols = flat(cotangent).astype(jnp.float32)
    grad_layer_scale2 = jnp.sum(upstream_cols * branch_cols, axis=0)
    grad_down_bias = jnp.sum(upstream_cols * layer_scale2, axis=0)

    tokens_all = flat(out_of_chunks(whole)).astype(jnp.float32)
    row_mean = jnp.mean(tokens_all, axis=-1, keepdims=True)
    centred = tokens_all - row_mean
    inv_std1 = lax.rsqrt(jnp.mean(centred * centred, axis=-1, keepdims=True) + EPS)
    normed1_cols = (flat(tokens).astype(jnp.float32) - row_mean) * inv_std1
    scaled = grad_lowered1 * cols(norm1_gain)
    row_sums = sum_small(
        [jnp.sum(scaled, axis=-1), jnp.sum(scaled * normed1_cols, axis=-1)], "tensor"
    )
    mean_scaled, mean_product = (values[:, None] / features for values in row_sums)
    input_grad = out_of_chunks([cols(part) for part in grad_residual]) + inv_std1 * (
        scaled - mean_scaled - normed1_cols * mean_product
    )

    grad_down_weight = sum_rows(grad_down_weight, order)
    grad_up_weight = sum_rows(grad_up_weight, swapped)
    grad_out_weight = sum_rows(grad_out_weight, order)
    middle = grad_qkv_weight.shape[0] // 2
    grad_qkv_weight = jnp.concatenate(
        [sum_rows(grad_qkv_weight[:middle], order), sum_rows(grad_qkv_weight[middle:], swapped)],
        axis=0,
    )
    small = [
        grad_query_bias,
        grad_value_bias,
        grad_out_bias,
        grad_layer_scale1,
        grad_norm2_gain,
        grad_norm2_bias,
        grad_up_bias,
        grad_down_bias,
        grad_layer_scale2,
    ]
    (
        grad_query_bias,
        grad_value_bias,
        grad_out_bias,
        grad_layer_scale1,
        grad_norm2_gain,
        grad_norm2_bias,
        grad_up_bias,
        grad_down_bias,
        grad_layer_scale2,
    ) = sum_small(small, "dp")
    norm1_sums = jnp.stack(
        sum_small(
            [jnp.sum(grad_lowered1 * normed1_cols, axis=0), jnp.sum(grad_lowered1, axis=0)], "dp"
        )
    )
    grad_norm1_gain, grad_norm1_bias = gather_near(gather_far(norm1_sums))
    output = unpad_rows(output)
    input_grad = unpad_rows(input_grad)
    return (
        output,
        input_grad,
        grad_norm1_gain,
        grad_norm1_bias,
        grad_qkv_weight,
        grad_query_bias,
        grad_value_bias,
        grad_out_weight,
        grad_out_bias,
        grad_layer_scale1,
        grad_norm2_gain,
        grad_norm2_bias,
        grad_up_weight,
        grad_up_bias,
        grad_down_weight,
        grad_down_bias,
        grad_layer_scale2,
    )


def solution(mesh):
    return jax.shard_map(
        shards,
        mesh=mesh,
        in_specs=(
            P("dp", "tensor"),
            P(),
            P(),
            P(None, "tensor"),
            P("tensor"),
            P("tensor"),
            P("tensor", None),
            P(),
            P(),
            P(),
            P(),
            P(None, "tensor"),
            P("tensor"),
            P("tensor", None),
            P("tensor"),
            P("tensor"),
            P("dp", "tensor"),
        ),
        out_specs=(
            P("dp", "tensor"),
            P("dp", "tensor"),
            P(),
            P(),
            P(None, "tensor"),
            P("tensor"),
            P("tensor"),
            P("tensor", None),
            P(),
            P(),
            P(),
            P(),
            P(None, "tensor"),
            P("tensor"),
            P("tensor", None),
            P("tensor"),
            P("tensor"),
        ),
        check_vma=False,
    )
```

```python
import math

import jax
import jax.numpy as jnp
from jax import lax
from jax.experimental import pallas as pl
from jax.experimental.pallas import tpu as pltpu
from jax.sharding import PartitionSpec as P

HD = 64
TOK_IMG = 257


EPS = 1e-06


def layer_norm(values, gain, bias):
    row_mean = jnp.mean(values, axis=-1, keepdims=True)
    centred = values - row_mean
    inv_std = lax.rsqrt(jnp.mean(centred * centred, axis=-1, keepdims=True) + EPS)
    normed = centred * inv_std
    return (normed, inv_std, normed * gain + bias)


def norm_back(upstream, normed, inv_std, gain):
    scaled = upstream * gain
    return inv_std * (
        scaled
        - jnp.mean(scaled, axis=-1, keepdims=True)
        - normed * jnp.mean(scaled * normed, axis=-1, keepdims=True)
    )


def gelu_parts(hidden_pre):
    cdf_value = 0.5 * (1.0 + jax.scipy.special.erf(hidden_pre * 2.0 ** (-0.5)))
    density = jnp.exp(-0.5 * hidden_pre * hidden_pre) * (2.0 * math.pi) ** (-0.5)
    return (hidden_pre * cdf_value, cdf_value + hidden_pre * density)


def contract_rows(left, right):
    return lax.dot_general(
        left, right, (((0,), (0,)), ((), ())), preferred_element_type=jnp.float32
    )


def contract_cols(left, right):
    return lax.dot_general(
        left, right, (((1,), (1,)), ((), ())), preferred_element_type=jnp.float32
    )


HEAD_COLS = 3 * HD
VMEM_BYTES = 48 << 20


def probs_of(packed, head, keep):
    start = head * HEAD_COLS
    query = packed[:, start : start + HD]
    key = packed[:, start + HD : start + 2 * HD]
    value = packed[:, start + 2 * HD : start + 3 * HD]
    scores = jnp.where(keep, contract_cols(key, query) * HD ** (-0.5), -1e30)
    powers = jnp.exp(scores - jnp.max(scores, axis=0, keepdims=True))
    probs = powers * (1.0 / jnp.sum(powers, axis=0, keepdims=True))
    return query, key, value, probs


def forward_kernel(
    tokens, gain, bias, weight, proj_bias, out_mine, out_theirs, low, packed, mixed, mine, theirs
):
    rows = tokens.shape[1]
    _, _, scaled = layer_norm(tokens[0].astype(jnp.float32), gain[...], bias[...])
    low[0] = scaled.astype(jnp.bfloat16)
    projected = jnp.dot(low[0], weight[...], preferred_element_type=jnp.float32)
    packed[0] = (projected + proj_bias[...]).astype(jnp.bfloat16)
    keep = lax.broadcasted_iota(jnp.int32, (rows, rows), 0) < TOK_IMG
    columns = packed[0]
    outs = []
    for head in range(weight.shape[1] // HEAD_COLS):
        _, _, value, probs = probs_of(columns, head, keep)
        outs.append(
            jnp.dot(
                value.astype(jnp.float32).T.astype(jnp.bfloat16),
                probs.astype(jnp.bfloat16),
                preferred_element_type=jnp.float32,
            )
        )
    mixed[0] = jnp.concatenate(outs, axis=0).T.astype(jnp.bfloat16)
    for part, out_weight in ((mine, out_mine), (theirs, out_theirs)):
        part[0] = jnp.dot(
            mixed[0], out_weight[...], preferred_element_type=jnp.float32
        ).astype(jnp.bfloat16)


def backward_kernel(
    core, tokens, attended_low, low2_mine, low2_theirs, cotangent, vectors, packed, out_weight,
    back_mine, back_theirs, residual_grad, upstream, grad, mine, theirs, query_sum, value_sum,
    feature_sums,
):
    rows = packed.shape[1]
    heads = packed.shape[2] // HEAD_COLS

    @pl.when(pl.program_id(0) == 0)
    def _():
        query_sum[...] = jnp.zeros_like(query_sum)
        value_sum[...] = jnp.zeros_like(value_sum)
        feature_sums[...] = jnp.zeros_like(feature_sums)

    attended = attended_low[0].astype(jnp.float32) + vectors[0:1]
    residual = tokens[0].astype(jnp.float32) + vectors[1:2] * attended
    normed, inv_std, _ = layer_norm(residual, vectors[2:3], vectors[3:4])
    grad_low2 = rejoin(core[0] == 1, low2_mine, low2_theirs)
    grad_residual = cotangent[0].astype(jnp.float32) + norm_back(
        grad_low2, normed, inv_std, vectors[2:3]
    )
    residual_grad[0] = grad_residual
    grad_attended = grad_residual * vectors[1:2]
    upstream[0] = grad_attended.astype(jnp.bfloat16)
    for row, product in enumerate(
        (grad_low2 * normed, grad_low2, grad_residual * attended, grad_attended)
    ):
        feature_sums[row : row + 1] += jnp.sum(product, axis=0, keepdims=True)
    grad_mixed = contract_cols(upstream[0], out_weight[...]).astype(jnp.bfloat16)
    keep = lax.broadcasted_iota(jnp.int32, (rows, rows), 0) < TOK_IMG
    columns = packed[0]
    queries = []
    for head in range(heads):
        query, key, value, probs = probs_of(columns, head, keep)
        grad_head = grad_mixed[:, head * HD : (head + 1) * HD]
        grad_probs = contract_cols(value, grad_head)
        delta = jnp.sum(probs * grad_probs, axis=0, keepdims=True)
        grad_scores = (probs * (grad_probs - delta) * HD ** (-0.5)).astype(jnp.bfloat16)
        grad_value = jnp.dot(
            probs.astype(jnp.bfloat16), grad_head, preferred_element_type=jnp.float32
        )
        grad_key = jnp.dot(grad_scores, query, preferred_element_type=jnp.float32)
        queries.append(
            jnp.dot(
                key.astype(jnp.float32).T.astype(jnp.bfloat16),
                grad_scores,
                preferred_element_type=jnp.float32,
            )
        )
        start = head * HEAD_COLS
        grad[0, :, start + HD : start + 2 * HD] = grad_key.astype(jnp.bfloat16)
        grad[0, :, start + 2 * HD : start + 3 * HD] = grad_value.astype(jnp.bfloat16)
        value_sum[:, head * HD : (head + 1) * HD] += jnp.sum(grad_value, axis=0, keepdims=True)
    grad_query = jnp.concatenate(queries, axis=0).T
    query_sum[...] += jnp.sum(grad_query, axis=0, keepdims=True)
    for head in range(heads):
        start = head * HEAD_COLS
        grad[0, :, start : start + HD] = grad_query[:, head * HD : (head + 1) * HD].astype(
            jnp.bfloat16
        )
    for part, weight in ((mine, back_mine), (theirs, back_theirs)):
        part[0] = contract_cols(grad[0], weight[...]).astype(jnp.bfloat16)


def rejoin(upper, mine, theirs):
    own, other = mine[0].astype(jnp.float32), theirs[0].astype(jnp.float32)
    return jnp.concatenate(
        [jnp.where(upper, other, own), jnp.where(upper, own, other)], axis=-1
    )


def hidden_kernel(
    core, tokens, mine, theirs, upstream, vectors, up_weight, up_bias, down_weight, up_mine,
    up_theirs, attended_low, low, activated_low, branch_grad, grad_low, part_mine, part_theirs,
    bias_sum,
):
    @pl.when(pl.program_id(0) == 0)
    def _():
        bias_sum[...] = jnp.zeros_like(bias_sum)

    joined = rejoin(core[0] == 1, mine, theirs)
    attended_low[0] = joined.astype(jnp.bfloat16)
    residual = tokens[0].astype(jnp.float32) + vectors[1:2] * (joined + vectors[0:1])
    _, _, scaled = layer_norm(residual, vectors[2:3], vectors[3:4])
    low[0] = scaled.astype(jnp.bfloat16)
    branch_grad[0] = (upstream[0].astype(jnp.float32) * vectors[4:5]).astype(jnp.bfloat16)
    hidden_pre = jnp.dot(low[0], up_weight[...], preferred_element_type=jnp.float32) + up_bias[...]
    activated, slope = gelu_parts(hidden_pre)
    activated_low[0] = activated.astype(jnp.bfloat16)
    grad_pre = contract_cols(branch_grad[0], down_weight[...]) * slope
    bias_sum[...] += jnp.sum(grad_pre, axis=0, keepdims=True)
    grad_low[0] = grad_pre.astype(jnp.bfloat16)
    for part, weight in ((part_mine, up_mine), (part_theirs, up_theirs)):
        part[0] = contract_cols(grad_low[0], weight[...]).astype(jnp.bfloat16)


def per_image(shape):
    return pl.BlockSpec((1,) + shape[1:], lambda image: (image, 0, 0))


def resident(shape):
    return pl.BlockSpec(shape, lambda image: (0, 0))


def run_images(kernel, args, outs, name, core=None):
    images = next(arg.shape[0] for arg in args if arg.ndim == 3)
    spec = lambda shape: per_image(shape) if len(shape) == 3 else resident(shape)
    in_specs = [spec(arg.shape) for arg in args]
    if core is not None:
        in_specs = [pl.BlockSpec(memory_space=pltpu.SMEM)] + in_specs
        args = (core,) + tuple(args)
    return pl.pallas_call(
        kernel,
        grid=(images,),
        in_specs=in_specs,
        out_specs=[spec(out.shape) for out in outs],
        out_shape=outs,
        compiler_params=pltpu.CompilerParams(vmem_limit_bytes=VMEM_BYTES),
        name=name,
    )(*args)


def low_of(like, width):
    return jax.ShapeDtypeStruct(like.shape[:2] + (width,), jnp.bfloat16)


def total_of(rows, width):
    return jax.ShapeDtypeStruct((rows, width), jnp.float32)


def attention_forward(tokens, gain, bias, weight, proj_bias, out_mine, out_theirs):
    half = out_mine.shape[1]
    widths = (tokens.shape[2], weight.shape[1], out_mine.shape[0], half, half)
    outs = [low_of(tokens, width) for width in widths]
    args = (tokens, gain, bias, weight, proj_bias, out_mine, out_theirs)
    return run_images(forward_kernel, args, outs, "attention_forward")


def hidden_both(core, tokens, *args):
    mine, up_weight = args[0], args[4]
    features, units, half = tokens.shape[2], up_weight.shape[1], mine.shape[2]
    widths = (features, features, units, features, units, half, half)
    outs = [low_of(tokens, width) for width in widths] + [total_of(1, units)]
    return run_images(hidden_kernel, (tokens,) + args, outs, "hidden_both", core)


def attention_backward(core, tokens, *args):
    packed, back_mine = args[5], args[7]
    features, width, half = tokens.shape[2], packed.shape[2], back_mine.shape[0]
    outs = [jax.ShapeDtypeStruct(tokens.shape, jnp.float32)]
    outs += [low_of(tokens, columns) for columns in (features, width, half, half)]
    outs += [total_of(1, width // 3), total_of(1, width // 3), total_of(4, features)]
    return run_images(backward_kernel, (tokens,) + args, outs, "attention_backward", core)


def exchange(block, axis, bit):
    size = lax.axis_size(axis)
    return lax.ppermute(block, axis, [(index, index ^ (1 << bit)) for index in range(size)])


def bit_of(axis, bit):
    return (lax.axis_index(axis) >> bit) % 2 == 1


def bits_in(axis):
    return (lax.axis_size(axis) - 1).bit_length()


def after(value, *others):
    return lax.optimization_barrier((value, *others))[0]


def split_blocks(values, dim):
    count = lax.axis_size("tensor")
    blocks = jnp.split(values, count, axis=dim)
    even = jnp.concatenate(blocks[0::2], axis=dim)
    odd = jnp.concatenate(blocks[1::2], axis=dim)
    upper = bit_of("tensor", 0)
    return jnp.where(upper, odd, even), jnp.where(upper, even, odd)


def split_halves(values, dim):
    low, high = jnp.split(values, 2, axis=dim)
    upper = bit_of("tensor", 0)
    return jnp.where(upper, high, low), jnp.where(upper, low, high)


def join_blocks(mine, theirs):
    count = lax.axis_size("tensor") // 2
    upper = bit_of("tensor", 0)
    pieces = []
    for own, other in zip(jnp.split(mine, count, axis=-1), jnp.split(theirs, count, axis=-1)):
        pieces += [jnp.where(upper, other, own), jnp.where(upper, own, other)]
    return jnp.concatenate(pieces, axis=-1)


def gather_far(block):
    for bit in range(1, bits_in("tensor")):
        got = exchange(block, "tensor", bit)
        upper = bit_of("tensor", bit)
        block = jnp.concatenate(
            [jnp.where(upper, got, block), jnp.where(upper, block, got)], axis=-1
        )
    return block


def gather_near(block):
    return join_blocks(block, exchange(block, "tensor", 0))


def add_near(mine, theirs):
    return mine.astype(jnp.float32) + exchange(theirs, "tensor", 0).astype(jnp.float32)


def add_far(total):
    for bit in range(1, bits_in("tensor")):
        sent = total.astype(jnp.bfloat16)
        total = sent.astype(jnp.float32) + exchange(sent, "tensor", bit).astype(jnp.float32)
    return total.astype(jnp.bfloat16)


def scatter_far(total):
    for bit in reversed(range(1, bits_in("tensor"))):
        low, high = jnp.split(total, 2, axis=-1)
        upper = bit_of("tensor", bit)
        got = exchange(jnp.where(upper, low, high).astype(jnp.bfloat16), "tensor", bit)
        total = jnp.where(upper, high, low) + got.astype(jnp.float32)
    return total


def halve_rows(grad, bit):
    low, high = jnp.split(grad, 2, axis=0)
    upper = bit_of("dp", bit)
    got = exchange(jnp.where(upper, low, high).astype(jnp.bfloat16), "dp", bit)
    return jnp.where(upper, high, low) + got.astype(jnp.float32)


def double_rows(grad, bit):
    got = exchange(grad, "dp", bit)
    upper = bit_of("dp", bit)
    return jnp.concatenate([jnp.where(upper, got, grad), jnp.where(upper, grad, got)], axis=0)


def sum_rows(grad, order):
    for bit in order:
        grad = halve_rows(grad, bit)
    grad = grad.astype(jnp.bfloat16)
    for bit in reversed(order):
        grad = double_rows(grad, bit)
    return grad.astype(jnp.float32)


def sum_small(values, axis):
    packed = jnp.concatenate(values)
    for bit in range(bits_in(axis)):
        packed = packed + exchange(packed, axis, bit)
    result, start = [], 0
    for value in values:
        result.append(packed[start : start + value.shape[0]])
        start += value.shape[0]
    return result


def shards(
    tokens,
    norm1_gain,
    norm1_bias,
    qkv_weight,
    query_bias,
    value_bias,
    out_weight,
    out_bias,
    layer_scale1,
    norm2_gain,
    norm2_bias,
    up_weight,
    up_bias,
    down_weight,
    down_bias,
    layer_scale2,
    cotangent,
):
    images = tokens.shape[0] // TOK_IMG
    width_local = tokens.shape[1]
    features = norm1_gain.shape[0]
    padded = -(-TOK_IMG // 8) * 8
    heads_local = query_bias.shape[0] // HD
    chunks = 2 if images % 2 == 0 else 1
    col_start = lax.axis_index("tensor") * width_local
    order = tuple(range(bits_in("dp")))
    swapped = order[1:2] + order[:1] + order[2:]

    def cols(values):
        return lax.dynamic_slice_in_dim(values, col_start, width_local, values.ndim - 1)

    def pad_rows(values):
        values = values.reshape(images, TOK_IMG, width_local)
        return jnp.pad(values, ((0, 0), (0, padded - TOK_IMG), (0, 0)))

    def flat(values):
        return values.reshape(-1, values.shape[-1])

    def unpad_rows(values):
        values = values.reshape(images, padded, width_local)
        return values[:, :TOK_IMG].reshape(images * TOK_IMG, width_local)

    def in_chunks(values):
        return jnp.split(values, chunks, axis=0)

    def out_of_chunks(values):
        return jnp.concatenate(values, axis=0)

    tokens = pad_rows(tokens)
    cotangent = pad_rows(cotangent)
    core = (lax.axis_index("tensor") % 2).astype(jnp.int32).reshape(1)
    proj_bias = jnp.stack(
        [
            query_bias.reshape(heads_local, HD),
            jnp.zeros((heads_local, HD), jnp.float32),
            value_bias.reshape(heads_local, HD),
        ],
        axis=1,
    ).reshape(1, 3 * heads_local * HD)
    tokens_far = [gather_far(part) for part in in_chunks(tokens)]
    out_mine, out_theirs = split_halves(out_weight, 1)
    whole = [gather_near(part) for part in tokens_far]
    cotangent_far = gather_far(after(cotangent, *tokens_far))
    scale2_all = gather_near(gather_far(layer_scale2[None]))
    forward = [
        attention_forward(
            part, norm1_gain[None], norm1_bias[None], qkv_weight, proj_bias, out_mine, out_theirs
        )
        for part in whole
    ]
    upstream = in_chunks(gather_near(cotangent_far))
    up_mine, up_theirs = split_halves(up_weight, 0)
    vectors = jnp.concatenate(
        [out_bias[None], layer_scale1[None], norm2_gain[None], norm2_bias[None], scale2_all]
    )

    hidden = []
    for index in range(chunks):
        mine = add_far(add_near(*forward[index][3:5]))
        theirs = exchange(mine, "tensor", 0)
        hidden.append(
            hidden_both(
                core,
                whole[index],
                mine,
                theirs,
                upstream[index],
                vectors,
                up_weight,
                up_bias[None],
                down_weight,
                up_mine,
                up_theirs,
            )
        )
    every = lambda index: flat(out_of_chunks([parts[index] for parts in hidden]))
    activated_all = every(2)
    grad_down_weight = contract_rows(activated_all, every(3))
    grad_up_weight = contract_rows(every(1), every(4))
    grad_up_bias = sum(parts[7] for parts in hidden)[0]

    qkv_mine, qkv_theirs = split_blocks(qkv_weight, 0)
    back = []
    for index in range(chunks):
        mine = add_far(add_near(*hidden[index][5:7]))
        theirs = exchange(mine, "tensor", 0)
        back.append(
            attention_backward(
                core,
                whole[index],
                hidden[index][0],
                mine,
                theirs,
                upstream[index],
                vectors,
                forward[index][1],
                out_weight,
                qkv_mine,
                qkv_theirs,
            )
        )
    grad_norm2_gain, grad_norm2_bias, grad_layer_scale1, grad_out_bias = sum(
        parts[7] for parts in back
    )
    grad_query_bias = sum(parts[5] for parts in back)[0]
    grad_value_bias = sum(parts[6] for parts in back)[0]
    grad_out_weight = contract_rows(
        flat(out_of_chunks([parts[2] for parts in forward])),
        flat(out_of_chunks([parts[1] for parts in back])),
    )
    grad_qkv_weight = contract_rows(
        flat(out_of_chunks([parts[0] for parts in forward])),
        flat(out_of_chunks([parts[2] for parts in back])),
    )
    grad_lowered1 = out_of_chunks(
        [scatter_far(add_near(flat(parts[3]), flat(parts[4]))) for parts in back]
    )

    down_mine, down_theirs = split_blocks(down_weight, 1)
    branch_cols = (
        scatter_far(
            add_near(
                jnp.dot(
                    activated_all, down_mine, preferred_element_type=jnp.float32
                ).astype(jnp.bfloat16),
                jnp.dot(
                    activated_all, down_theirs, preferred_element_type=jnp.float32
                ).astype(jnp.bfloat16),
            )
        )
        + down_bias
    )
    attended_cols = flat(out_of_chunks([cols(parts[0]) for parts in hidden])).astype(jnp.float32)
    residual_cols = flat(tokens).astype(jnp.float32) + cols(layer_scale1) * (
        attended_cols + cols(out_bias)
    )
    output = residual_cols + layer_scale2 * branch_cols
    upstream_cols = flat(cotangent).astype(jnp.float32)
    grad_layer_scale2 = jnp.sum(upstream_cols * branch_cols, axis=0)
    grad_down_bias = jnp.sum(upstream_cols * layer_scale2, axis=0)

    tokens_all = flat(out_of_chunks(whole)).astype(jnp.float32)
    row_mean = jnp.mean(tokens_all, axis=-1, keepdims=True)
    centred = tokens_all - row_mean
    inv_std1 = lax.rsqrt(jnp.mean(centred * centred, axis=-1, keepdims=True) + EPS)
    normed1_cols = (flat(tokens).astype(jnp.float32) - row_mean) * inv_std1
    scaled = grad_lowered1 * cols(norm1_gain)
    row_sums = sum_small(
        [jnp.sum(scaled, axis=-1), jnp.sum(scaled * normed1_cols, axis=-1)], "tensor"
    )
    mean_scaled, mean_product = (values[:, None] / features for values in row_sums)
    input_grad = flat(out_of_chunks([cols(parts[0]) for parts in back])) + inv_std1 * (
        scaled - mean_scaled - normed1_cols * mean_product
    )

    grad_down_weight = sum_rows(grad_down_weight, order)
    grad_up_weight = sum_rows(grad_up_weight, swapped)
    grad_out_weight = sum_rows(grad_out_weight, order)
    middle = grad_qkv_weight.shape[0] // 2
    grad_qkv_weight = jnp.concatenate(
        [sum_rows(grad_qkv_weight[:middle], order), sum_rows(grad_qkv_weight[middle:], swapped)],
        axis=0,
    )
    small = [
        grad_query_bias,
        grad_value_bias,
        grad_out_bias,
        grad_layer_scale1,
        grad_norm2_gain,
        grad_norm2_bias,
        grad_up_bias,
        grad_down_bias,
        grad_layer_scale2,
    ]
    (
        grad_query_bias,
        grad_value_bias,
        grad_out_bias,
        grad_layer_scale1,
        grad_norm2_gain,
        grad_norm2_bias,
        grad_up_bias,
        grad_down_bias,
        grad_layer_scale2,
    ) = sum_small(small, "dp")
    norm1_sums = jnp.stack(
        sum_small(
            [jnp.sum(grad_lowered1 * normed1_cols, axis=0), jnp.sum(grad_lowered1, axis=0)], "dp"
        )
    )
    grad_norm1_gain, grad_norm1_bias = gather_near(gather_far(norm1_sums))
    output = unpad_rows(output)
    input_grad = unpad_rows(input_grad)
    return (
        output,
        input_grad,
        grad_norm1_gain,
        grad_norm1_bias,
        grad_qkv_weight,
        grad_query_bias,
        grad_value_bias,
        grad_out_weight,
        grad_out_bias,
        grad_layer_scale1,
        grad_norm2_gain,
        grad_norm2_bias,
        grad_up_weight,
        grad_up_bias,
        grad_down_weight,
        grad_down_bias,
        grad_layer_scale2,
    )


def solution(mesh):
    return jax.shard_map(
        shards,
        mesh=mesh,
        in_specs=(
            P("dp", "tensor"),
            P(),
            P(),
            P(None, "tensor"),
            P("tensor"),
            P("tensor"),
            P("tensor", None),
            P(),
            P(),
            P(),
            P(),
            P(None, "tensor"),
            P("tensor"),
            P("tensor", None),
            P("tensor"),
            P("tensor"),
            P("dp", "tensor"),
        ),
        out_specs=(
            P("dp", "tensor"),
            P("dp", "tensor"),
            P(),
            P(),
            P(None, "tensor"),
            P("tensor"),
            P("tensor"),
            P("tensor", None),
            P(),
            P(),
            P(),
            P(),
            P(None, "tensor"),
            P("tensor"),
            P("tensor", None),
            P("tensor"),
            P("tensor"),
        ),
        check_vma=False,
    )
```

```python
import math

import jax
import jax.numpy as jnp
from jax import lax
from jax.experimental import pallas as pl
from jax.experimental.pallas import tpu as pltpu
from jax.sharding import PartitionSpec as P

HD = 64
TOK_IMG = 257


EPS = 1e-06


def layer_norm(values, gain, bias):
    row_mean = jnp.mean(values, axis=-1, keepdims=True)
    centred = values - row_mean
    inv_std = lax.rsqrt(jnp.mean(centred * centred, axis=-1, keepdims=True) + EPS)
    normed = centred * inv_std
    return (normed, inv_std, normed * gain + bias)


def norm_back(upstream, normed, inv_std, gain):
    scaled = upstream * gain
    return inv_std * (
        scaled
        - jnp.mean(scaled, axis=-1, keepdims=True)
        - normed * jnp.mean(scaled * normed, axis=-1, keepdims=True)
    )


def gelu_parts(hidden_pre):
    cdf_value = 0.5 * (1.0 + jax.scipy.special.erf(hidden_pre * 2.0 ** (-0.5)))
    density = jnp.exp(-0.5 * hidden_pre * hidden_pre) * (2.0 * math.pi) ** (-0.5)
    return (hidden_pre * cdf_value, cdf_value + hidden_pre * density)


def contract_rows(left, right):
    return lax.dot_general(
        left, right, (((0,), (0,)), ((), ())), preferred_element_type=jnp.float32
    )


def contract_cols(left, right):
    return lax.dot_general(
        left, right, (((1,), (1,)), ((), ())), preferred_element_type=jnp.float32
    )


HEAD_COLS = 3 * HD
VMEM_BYTES = 48 << 20


def probs_of(packed, head, keep):
    start = head * HEAD_COLS
    query = packed[:, start : start + HD]
    key = packed[:, start + HD : start + 2 * HD]
    value = packed[:, start + 2 * HD : start + 3 * HD]
    scores = jnp.where(keep, contract_cols(key, query) * HD ** (-0.5), -1e30)
    powers = jnp.exp(scores - jnp.max(scores, axis=0, keepdims=True))
    probs = powers * (1.0 / jnp.sum(powers, axis=0, keepdims=True))
    return query, key, value, probs


def forward_kernel(
    tokens, gain, bias, weight, proj_bias, out_mine, out_theirs, low, packed, mixed, mine, theirs
):
    rows = tokens.shape[1]
    _, _, scaled = layer_norm(tokens[0].astype(jnp.float32), gain[...], bias[...])
    low[0] = scaled.astype(jnp.bfloat16)
    projected = jnp.dot(low[0], weight[...], preferred_element_type=jnp.float32)
    packed[0] = (projected + proj_bias[...]).astype(jnp.bfloat16)
    keep = lax.broadcasted_iota(jnp.int32, (rows, rows), 0) < TOK_IMG
    columns = packed[0]
    outs = []
    for head in range(weight.shape[1] // HEAD_COLS):
        _, _, value, probs = probs_of(columns, head, keep)
        outs.append(
            jnp.dot(
                value.astype(jnp.float32).T.astype(jnp.bfloat16),
                probs.astype(jnp.bfloat16),
                preferred_element_type=jnp.float32,
            )
        )
    mixed[0] = jnp.concatenate(outs, axis=0).T.astype(jnp.bfloat16)
    for part, out_weight in ((mine, out_mine), (theirs, out_theirs)):
        part[0] = jnp.dot(
            mixed[0], out_weight[...], preferred_element_type=jnp.float32
        ).astype(jnp.bfloat16)


def backward_kernel(
    core, tokens, attended_low, low2_mine, low2_theirs, cotangent, vectors, packed, out_weight,
    back_mine, back_theirs, residual_grad, upstream, grad, mine, theirs, query_sum, value_sum,
    feature_sums,
):
    rows = packed.shape[1]
    heads = packed.shape[2] // HEAD_COLS

    @pl.when(pl.program_id(0) == 0)
    def _():
        query_sum[...] = jnp.zeros_like(query_sum)
        value_sum[...] = jnp.zeros_like(value_sum)
        feature_sums[...] = jnp.zeros_like(feature_sums)

    attended = attended_low[0].astype(jnp.float32) + vectors[0:1]
    residual = tokens[0].astype(jnp.float32) + vectors[1:2] * attended
    normed, inv_std, _ = layer_norm(residual, vectors[2:3], vectors[3:4])
    grad_low2 = rejoin(core[0] == 1, low2_mine, low2_theirs)
    grad_residual = cotangent[0].astype(jnp.float32) + norm_back(
        grad_low2, normed, inv_std, vectors[2:3]
    )
    residual_grad[0] = grad_residual
    grad_attended = grad_residual * vectors[1:2]
    upstream[0] = grad_attended.astype(jnp.bfloat16)
    for row, product in enumerate(
        (grad_low2 * normed, grad_low2, grad_residual * attended, grad_attended)
    ):
        feature_sums[row : row + 1] += jnp.sum(product, axis=0, keepdims=True)
    grad_mixed = contract_cols(upstream[0], out_weight[...]).astype(jnp.bfloat16)
    keep = lax.broadcasted_iota(jnp.int32, (rows, rows), 0) < TOK_IMG
    columns = packed[0]
    queries = []
    for head in range(heads):
        query, key, value, probs = probs_of(columns, head, keep)
        grad_head = grad_mixed[:, head * HD : (head + 1) * HD]
        grad_probs = contract_cols(value, grad_head)
        delta = jnp.sum(probs * grad_probs, axis=0, keepdims=True)
        grad_scores = (probs * (grad_probs - delta) * HD ** (-0.5)).astype(jnp.bfloat16)
        grad_value = jnp.dot(
            probs.astype(jnp.bfloat16), grad_head, preferred_element_type=jnp.float32
        )
        grad_key = jnp.dot(grad_scores, query, preferred_element_type=jnp.float32)
        queries.append(
            jnp.dot(
                key.astype(jnp.float32).T.astype(jnp.bfloat16),
                grad_scores,
                preferred_element_type=jnp.float32,
            )
        )
        start = head * HEAD_COLS
        grad[0, :, start + HD : start + 2 * HD] = grad_key.astype(jnp.bfloat16)
        grad[0, :, start + 2 * HD : start + 3 * HD] = grad_value.astype(jnp.bfloat16)
        value_sum[:, head * HD : (head + 1) * HD] += jnp.sum(grad_value, axis=0, keepdims=True)
    grad_query = jnp.concatenate(queries, axis=0).T
    query_sum[...] += jnp.sum(grad_query, axis=0, keepdims=True)
    for head in range(heads):
        start = head * HEAD_COLS
        grad[0, :, start : start + HD] = grad_query[:, head * HD : (head + 1) * HD].astype(
            jnp.bfloat16
        )
    for part, weight in ((mine, back_mine), (theirs, back_theirs)):
        part[0] = contract_cols(grad[0], weight[...]).astype(jnp.bfloat16)


def rejoin(upper, mine, theirs):
    own, other = mine[0].astype(jnp.float32), theirs[0].astype(jnp.float32)
    return jnp.concatenate(
        [jnp.where(upper, other, own), jnp.where(upper, own, other)], axis=-1
    )


def hidden_kernel(
    core, tokens, mine, theirs, upstream, vectors, up_weight, up_bias, down_weight, up_mine,
    up_theirs, attended_low, low, activated_low, branch_grad, grad_low, part_mine, part_theirs,
    bias_sum,
):
    @pl.when(pl.program_id(0) == 0)
    def _():
        bias_sum[...] = jnp.zeros_like(bias_sum)

    joined = rejoin(core[0] == 1, mine, theirs)
    attended_low[0] = joined.astype(jnp.bfloat16)
    residual = tokens[0].astype(jnp.float32) + vectors[1:2] * (joined + vectors[0:1])
    _, _, scaled = layer_norm(residual, vectors[2:3], vectors[3:4])
    low[0] = scaled.astype(jnp.bfloat16)
    branch_grad[0] = (upstream[0].astype(jnp.float32) * vectors[4:5]).astype(jnp.bfloat16)
    hidden_pre = jnp.dot(low[0], up_weight[...], preferred_element_type=jnp.float32) + up_bias[...]
    activated, slope = gelu_parts(hidden_pre)
    activated_low[0] = activated.astype(jnp.bfloat16)
    grad_pre = contract_cols(branch_grad[0], down_weight[...]) * slope
    bias_sum[...] += jnp.sum(grad_pre, axis=0, keepdims=True)
    grad_low[0] = grad_pre.astype(jnp.bfloat16)
    for part, weight in ((part_mine, up_mine), (part_theirs, up_theirs)):
        part[0] = contract_cols(grad_low[0], weight[...]).astype(jnp.bfloat16)


def run_images(kernel, base, args, outs, name, core=None, carried=()):
    images, total = args[0].shape[0], max(out.shape[0] for out in outs if len(out.shape) == 3)

    def spec(shape):
        if len(shape) == 2:
            return pl.BlockSpec(shape, lambda image: (0, 0))
        first = base if shape[0] == total else 0
        return pl.BlockSpec((1,) + shape[1:], lambda image: (image + first, 0, 0))

    in_specs = [spec(arg.shape) for arg in args]
    if core is not None:
        in_specs = [pl.BlockSpec(memory_space=pltpu.SMEM)] + in_specs
        args = (core,) + tuple(args)
    skipped, count = len(carried), len(args)

    def body(*refs):
        kernel(*refs[:count], *refs[count + skipped :])

    return pl.pallas_call(
        body,
        grid=(images,),
        in_specs=in_specs + [pl.BlockSpec(memory_space=pl.ANY)] * skipped,
        out_specs=[spec(out.shape) for out in outs],
        out_shape=outs,
        input_output_aliases={count + index: index for index in range(skipped)},
        compiler_params=pltpu.CompilerParams(vmem_limit_bytes=VMEM_BYTES),
        name=name,
    )(*args, *carried)


def low_of(images, rows, width):
    return jax.ShapeDtypeStruct((images, rows, width), jnp.bfloat16)


def total_of(rows, width):
    return jax.ShapeDtypeStruct((rows, width), jnp.float32)


def attention_forward(total, base, carried, tokens, gain, bias, weight, *args):
    chunk, rows, features = tokens.shape
    out_mine = args[1]
    half = out_mine.shape[1]
    widths = (features, weight.shape[1], out_mine.shape[0])
    outs = [low_of(total, rows, width) for width in widths]
    outs += [low_of(chunk, rows, half), low_of(chunk, rows, half)]
    args = (tokens, gain, bias, weight) + args
    return run_images(forward_kernel, base, args, outs, "attention_forward", None, carried)


def hidden_both(total, base, carried, core, tokens, mine, *args):
    chunk, rows, features = tokens.shape
    units, half = args[3].shape[1], mine.shape[2]
    widths = (features, features, units, features, units)
    outs = [low_of(total, rows, width) for width in widths]
    outs += [low_of(chunk, rows, half), low_of(chunk, rows, half), total_of(1, units)]
    args = (tokens, mine) + args
    return run_images(hidden_kernel, base, args, outs, "hidden_both", core, carried)


def attention_backward(total, base, carried, core, tokens, *args):
    chunk, rows, features = tokens.shape
    width, half = args[5].shape[2], args[7].shape[0]
    outs = [jax.ShapeDtypeStruct((total, rows, features), jnp.float32)]
    outs += [low_of(total, rows, columns) for columns in (features, width)]
    outs += [low_of(chunk, rows, half), low_of(chunk, rows, half)]
    outs += [total_of(1, width // 3), total_of(1, width // 3), total_of(4, features)]
    args = (tokens,) + args
    return run_images(backward_kernel, base, args, outs, "attention_backward", core, carried)


def exchange(block, axis, bit):
    size = lax.axis_size(axis)
    return lax.ppermute(block, axis, [(index, index ^ (1 << bit)) for index in range(size)])


def bit_of(axis, bit):
    return (lax.axis_index(axis) >> bit) % 2 == 1


def bits_in(axis):
    return (lax.axis_size(axis) - 1).bit_length()


def after(value, *others):
    return lax.optimization_barrier((value, *others))[0]


def split_blocks(values, dim):
    count = lax.axis_size("tensor")
    blocks = jnp.split(values, count, axis=dim)
    even = jnp.concatenate(blocks[0::2], axis=dim)
    odd = jnp.concatenate(blocks[1::2], axis=dim)
    upper = bit_of("tensor", 0)
    return jnp.where(upper, odd, even), jnp.where(upper, even, odd)


def split_halves(values, dim):
    low, high = jnp.split(values, 2, axis=dim)
    upper = bit_of("tensor", 0)
    return jnp.where(upper, high, low), jnp.where(upper, low, high)


def join_blocks(mine, theirs):
    count = lax.axis_size("tensor") // 2
    upper = bit_of("tensor", 0)
    pieces = []
    for own, other in zip(jnp.split(mine, count, axis=-1), jnp.split(theirs, count, axis=-1)):
        pieces += [jnp.where(upper, other, own), jnp.where(upper, own, other)]
    return jnp.concatenate(pieces, axis=-1)


def gather_far(block, others=()):
    for bit in range(1, bits_in("tensor")):
        got = after(exchange(block, "tensor", bit), others)
        upper = bit_of("tensor", bit)
        block = jnp.concatenate(
            [jnp.where(upper, got, block), jnp.where(upper, block, got)], axis=-1
        )
    return block


def gather_near(block):
    return join_blocks(block, exchange(block, "tensor", 0))


def add_near(mine, theirs, others=()):
    got = after(exchange(theirs, "tensor", 0), others)
    return (mine.astype(jnp.float32) + got.astype(jnp.float32)).astype(jnp.bfloat16)


def add_far(total, others=()):
    for bit in range(1, bits_in("tensor")):
        got = after(exchange(total, "tensor", bit), others)
        total = (total.astype(jnp.float32) + got.astype(jnp.float32)).astype(jnp.bfloat16)
    return total


def halve_send(grads, bit):
    upper = bit_of("dp", bit)
    kept, got = [], []
    for grad in grads:
        low, high = jnp.split(grad, 2, axis=0)
        got.append(exchange(jnp.where(upper, low, high).astype(jnp.bfloat16), "dp", bit))
        kept.append(jnp.where(upper, high, low))
    return kept, got


def halve_join(kept, got):
    return [mine + part.astype(jnp.float32) for mine, part in zip(kept, got)]


def double_send(grads, bit):
    return grads, [exchange(grad, "dp", bit) for grad in grads]


def double_join(grads, got, bit):
    upper = bit_of("dp", bit)
    return [
        jnp.concatenate([jnp.where(upper, part, grad), jnp.where(upper, grad, part)], axis=0)
        for grad, part in zip(grads, got)
    ]


def row_sums(flows):
    steps = len(flows[0][1])
    grads = [list(group) for group, _ in flows]
    for step in range(2 * steps):
        halving = step < steps
        bits = [order[step] if halving else order[2 * steps - 1 - step] for _, order in flows]
        if step == steps:
            grads = [[grad.astype(jnp.bfloat16) for grad in group] for group in grads]
        send = halve_send if halving else double_send
        sent = [send(group, bit) for group, bit in zip(grads, bits)]
        others = yield grads
        got = lax.optimization_barrier(([part for _, part in sent], others))[0]
        if halving:
            grads = [halve_join(kept, part) for (kept, _), part in zip(sent, got)]
        else:
            grads = [
                double_join(kept, part, bit) for (kept, _), part, bit in zip(sent, got, bits)
            ]
    yield [[grad.astype(jnp.float32) for grad in group] for group in grads]


def scatter_columns(results, name, parts):
    got = yield [exchange(theirs, "tensor", 0) for _, theirs in parts]
    totals = [
        flat(mine).astype(jnp.float32) + flat(part).astype(jnp.float32)
        for (mine, _), part in zip(parts, got)
    ]
    for bit in reversed(range(1, bits_in("tensor"))):
        upper = bit_of("tensor", bit)
        halves = [jnp.split(total, 2, axis=-1) for total in totals]
        got = yield [
            exchange(jnp.where(upper, low, high).astype(jnp.bfloat16), "tensor", bit)
            for low, high in halves
        ]
        totals = [
            jnp.where(upper, high, low) + part.astype(jnp.float32)
            for (low, high), part in zip(halves, got)
        ]
    results[name] = jnp.concatenate(totals, axis=0)


def sum_small(results, name, values, axis):
    packed = jnp.concatenate(values)
    for bit in range(bits_in(axis)):
        (got,) = yield [exchange(packed, axis, bit)]
        packed = packed + got
    sums, start = [], 0
    for value in values:
        sums.append(packed[start : start + value.shape[0]])
        start += value.shape[0]
    results[name] = sums


def gather_small(results, name, block):
    for bit in range(1, bits_in("tensor")):
        (got,) = yield [exchange(block, "tensor", bit)]
        upper = bit_of("tensor", bit)
        block = jnp.concatenate(
            [jnp.where(upper, got, block), jnp.where(upper, block, got)], axis=-1
        )
    (got,) = yield [exchange(block, "tensor", 0)]
    results[name] = join_blocks(block, got)


def flat(values):
    return values.reshape(-1, values.shape[-1])


class Tasks:
    def __init__(self):
        self.results, self.active = {}, []

    def add(self, task, name, *args):
        chain = task(self.results, name, *args)
        self.active.append((chain, next(chain)))

    def step(self, others):
        got = lax.optimization_barrier(([wanted for _, wanted in self.active], others))[0]
        chains, self.active = [chain for chain, _ in self.active], []
        for chain, arrived in zip(chains, got):
            try:
                self.active.append((chain, chain.send(arrived)))
            except StopIteration:
                pass
        return got


def merge_steps(steps):
    half = steps // 2
    hidden = ["hidden"] * (steps - 2)
    heads = ["heads"] * steps
    merged = heads[: half - 1] + hidden[: half - 1] + heads[:1] + hidden[:1]
    rest_heads, rest_hidden = heads[half:], hidden[half:]
    return merged + rest_heads[:1] + rest_hidden + rest_heads[1:]


def shards(
    tokens,
    norm1_gain,
    norm1_bias,
    qkv_weight,
    query_bias,
    value_bias,
    out_weight,
    out_bias,
    layer_scale1,
    norm2_gain,
    norm2_bias,
    up_weight,
    up_bias,
    down_weight,
    down_bias,
    layer_scale2,
    cotangent,
):
    images = tokens.shape[0] // TOK_IMG
    width_local = tokens.shape[1]
    features = norm1_gain.shape[0]
    padded = -(-TOK_IMG // 8) * 8
    heads_local = query_bias.shape[0] // HD
    chunks = 2 if images % 2 == 0 else 1
    col_start = lax.axis_index("tensor") * width_local

    def cols(values):
        return lax.dynamic_slice_in_dim(values, col_start, width_local, values.ndim - 1)

    def pad_rows(values):
        values = values.reshape(images, TOK_IMG, width_local)
        return jnp.pad(values, ((0, 0), (0, padded - TOK_IMG), (0, 0)))

    def unpad_rows(values):
        values = values.reshape(images, padded, width_local)
        return values[:, :TOK_IMG].reshape(images * TOK_IMG, width_local)

    def in_chunks(values):
        return jnp.split(values, chunks, axis=0)

    def out_of_chunks(values):
        return jnp.concatenate(values, axis=0)

    count = images // chunks
    core = (lax.axis_index("tensor") % 2).astype(jnp.int32).reshape(1)
    proj_bias = jnp.stack(
        [
            query_bias.reshape(heads_local, HD),
            jnp.zeros((heads_local, HD), jnp.float32),
            value_bias.reshape(heads_local, HD),
        ],
        axis=1,
    ).reshape(1, 3 * heads_local * HD)
    tokens = pad_rows(tokens)
    cotangent = pad_rows(cotangent)
    token_parts = in_chunks(tokens)
    out_mine, out_theirs = split_halves(out_weight, 1)
    far = gather_far(token_parts[0])
    later = lax.optimization_barrier((token_parts[1:], cotangent, far))
    token_parts[1:], cotangent_sent = later[:2]
    cotangent_far = gather_far(cotangent_sent)
    whole, forward, carried, attended, given = [], [], (), [], ()
    for index in range(chunks):
        joined = gather_near(far if index == 0 else gather_far(token_parts[index], given))
        whole.append(after(joined, attended))
        parts = attention_forward(
            images,
            index * count,
            carried,
            whole[index],
            norm1_gain[None],
            norm1_bias[None],
            qkv_weight,
            proj_bias,
            out_mine,
            out_theirs,
        )
        carried, given = parts[:3], parts[3:5]
        forward.append(parts)
        attended.append(add_near(*given))
    packed = carried[1]
    lowered1, mixed = flat(carried[0]), flat(carried[2])
    up_weight_late, scale2_late = after((up_weight, layer_scale2), attended)
    upstream = in_chunks(gather_near(after(cotangent_far, attended)))
    up_mine, up_theirs = split_halves(up_weight_late, 0)
    scale2_all = gather_near(gather_far(scale2_late[None]))
    vectors = jnp.concatenate(
        [out_bias[None], layer_scale1[None], norm2_gain[None], norm2_bias[None], scale2_all]
    )

    hidden, carried, low2, given = [], (), [], (vectors, up_mine, up_theirs, upstream)
    for index in range(chunks):
        mine = add_far(attended[index], given)
        theirs = exchange(mine, "tensor", 0)
        parts = hidden_both(
            images,
            index * count,
            carried,
            core,
            whole[index],
            after(mine, low2),
            theirs,
            upstream[index],
            vectors,
            up_weight,
            up_bias[None],
            down_weight,
            up_mine,
            up_theirs,
        )
        carried, given = parts[:5], parts[5:7]
        hidden.append(parts)
        if index < chunks - 1:
            low2.append(add_near(*given))
    attended_low = carried[0]
    lowered2, activated_low, branch_grad, grad_pre_low = (flat(part) for part in carried[1:])
    grad_up_bias = sum(parts[7] for parts in hidden)[0]
    grad_down_weight = contract_rows(activated_low, branch_grad)
    low2.append(add_near(*given, grad_down_weight))
    grad_up_weight = contract_rows(after(lowered2, low2), grad_pre_low)
    first_order = tuple(range(bits_in("dp")))
    second_order = first_order[1:2] + first_order[:1] + first_order[2:]
    hidden_sums = row_sums([([grad_down_weight], first_order), ([grad_up_weight], second_order)])
    next(hidden_sums)

    activated_late, qkv_late, down_late = after(
        (activated_low, qkv_weight, down_weight), grad_up_weight
    )
    qkv_mine, qkv_theirs = split_blocks(qkv_late, 0)
    branch_parts = [
        jnp.dot(activated_late, weight, preferred_element_type=jnp.float32).astype(jnp.bfloat16)
        for weight in split_blocks(down_late, 1)
    ]
    tasks = Tasks()
    results = tasks.results
    tasks.add(scatter_columns, "branch", [branch_parts])
    back, carried, given = [], (), (qkv_mine, qkv_theirs, branch_parts)
    for index in range(chunks):
        mine = add_far(low2[index], given)
        theirs = exchange(mine, "tensor", 0)
        parts = attention_backward(
            images,
            index * count,
            carried,
            core,
            whole[index],
            attended_low,
            mine,
            theirs,
            upstream[index],
            vectors,
            packed,
            out_weight,
            qkv_mine,
            qkv_theirs,
        )
        carried, given = parts[:3], parts[3:5]
        back.append(parts)
    residual_grad, grad_attended, grad_projected = (flat(part) for part in carried)
    tasks.add(scatter_columns, "lowered1", [parts[3:5] for parts in back])
    state = hidden_sums.send(given)
    grad_attended, grad_projected = after((grad_attended, grad_projected), state)
    grad_out_weight = contract_rows(mixed, grad_attended)
    grad_qkv_weight = contract_rows(lowered1, grad_projected)
    state = tasks.step((grad_out_weight, grad_qkv_weight))
    state = hidden_sums.send(state)
    rows = grad_qkv_weight.shape[0]
    first_rows = 3 * rows // 8
    grad_out_weight, grad_qkv_weight = after((grad_out_weight, grad_qkv_weight), state)
    heads_sums = row_sums(
        [
            ([grad_out_weight, grad_qkv_weight[:first_rows]], first_order),
            ([grad_qkv_weight[first_rows:]], second_order),
        ]
    )
    last = next(heads_sums)

    def finish(others):
        if "branch" in results and "output" not in results:
            branch_cols = results["branch"] + down_bias
            own, upstream_own, attended_own = after(
                (flat(tokens), flat(cotangent), attended_low), results["branch"]
            )
            attended_cols = cols(flat(attended_own)).astype(jnp.float32) + cols(out_bias)
            residual_cols = own.astype(jnp.float32) + cols(layer_scale1) * attended_cols
            results["output"] = unpad_rows(residual_cols + layer_scale2 * branch_cols)
            upstream_cols = upstream_own.astype(jnp.float32)
            results["scale2"] = jnp.sum(upstream_cols * branch_cols, axis=0)
            results["down_bias"] = jnp.sum(upstream_cols * layer_scale2, axis=0)
        if "lowered1" in results and "scaled" not in results:
            grad_lowered1 = results["lowered1"]
            own, every = after((flat(tokens), whole), grad_lowered1)
            tokens_all = flat(out_of_chunks(every)).astype(jnp.float32)
            row_mean = jnp.mean(tokens_all, axis=-1, keepdims=True)
            centred = tokens_all - row_mean
            inv_std1 = lax.rsqrt(jnp.mean(centred * centred, axis=-1, keepdims=True) + EPS)
            normed1 = (own.astype(jnp.float32) - row_mean) * inv_std1
            scaled = grad_lowered1 * cols(norm1_gain)
            results["scaled"] = (scaled, normed1, inv_std1)
            tasks.add(
                sum_small,
                "row_totals",
                [jnp.sum(scaled, axis=-1), jnp.sum(scaled * normed1, axis=-1)],
                "tensor",
            )
            results["norm1"] = [
                jnp.sum(grad_lowered1 * normed1, axis=0),
                jnp.sum(grad_lowered1, axis=0),
            ]
        if "norm1" in results and "output" in results and "packed" not in results:
            feature_sums = sum(parts[7] for parts in back)
            results["packed"] = [
                sum(parts[5] for parts in back)[0],
                sum(parts[6] for parts in back)[0],
                feature_sums[3],
                feature_sums[2],
                feature_sums[0],
                feature_sums[1],
                grad_up_bias,
                results["down_bias"],
                results["scale2"],
            ] + results["norm1"]
            tasks.add(sum_small, "small", results["packed"], "dp")
        if "row_totals" in results and "input_grad" not in results:
            scaled, normed1, inv_std1 = results["scaled"]
            mean_scaled, mean_product = (
                values[:, None] / features for values in results["row_totals"]
            )
            results["input_grad"] = unpad_rows(
                cols(residual_grad) + inv_std1 * (scaled - mean_scaled - normed1 * mean_product)
            )
        if "small" in results and "norm1_sums" not in results:
            results["norm1_sums"] = None
            tasks.add(gather_small, "norm1_all", jnp.stack(results["small"][9:]))

    finished = {}
    for name in merge_steps(2 * len(first_order)):
        if tasks.active:
            last = tasks.step(last)
            finish(last)
        last = (hidden_sums if name == "hidden" else heads_sums).send(last)
        finished[name] = last
    while tasks.active:
        last = tasks.step(last)
        finish(last)
    ((grad_down_weight,), (grad_up_weight,)) = finished["hidden"]
    ((grad_out_weight, top), (bottom,)) = finished["heads"]
    grad_qkv_weight = jnp.concatenate([top, bottom], axis=0)
    (
        grad_query_bias,
        grad_value_bias,
        grad_out_bias,
        grad_layer_scale1,
        grad_norm2_gain,
        grad_norm2_bias,
        grad_up_bias,
        grad_down_bias,
        grad_layer_scale2,
    ) = results["small"][:9]
    grad_norm1_gain, grad_norm1_bias = results["norm1_all"]
    output, input_grad = results["output"], results["input_grad"]
    return (
        output,
        input_grad,
        grad_norm1_gain,
        grad_norm1_bias,
        grad_qkv_weight,
        grad_query_bias,
        grad_value_bias,
        grad_out_weight,
        grad_out_bias,
        grad_layer_scale1,
        grad_norm2_gain,
        grad_norm2_bias,
        grad_up_weight,
        grad_up_bias,
        grad_down_weight,
        grad_down_bias,
        grad_layer_scale2,
    )


def solution(mesh):
    return jax.shard_map(
        shards,
        mesh=mesh,
        in_specs=(
            P("dp", "tensor"),
            P(),
            P(),
            P(None, "tensor"),
            P("tensor"),
            P("tensor"),
            P("tensor", None),
            P(),
            P(),
            P(),
            P(),
            P(None, "tensor"),
            P("tensor"),
            P("tensor", None),
            P("tensor"),
            P("tensor"),
            P("dp", "tensor"),
        ),
        out_specs=(
            P("dp", "tensor"),
            P("dp", "tensor"),
            P(),
            P(),
            P(None, "tensor"),
            P("tensor"),
            P("tensor"),
            P("tensor", None),
            P(),
            P(),
            P(),
            P(),
            P(None, "tensor"),
            P("tensor"),
            P("tensor", None),
            P("tensor"),
            P("tensor"),
        ),
        check_vma=False,
    )
```

```python
import math

import jax
import jax.numpy as jnp
from jax import lax
from jax.experimental import pallas as pl
from jax.experimental.pallas import tpu as pltpu
from jax.sharding import PartitionSpec as P

HD = 64
TOK_IMG = 257


EPS = 1e-06


def layer_norm(values, gain, bias):
    row_mean = jnp.mean(values, axis=-1, keepdims=True)
    centred = values - row_mean
    inv_std = lax.rsqrt(jnp.mean(centred * centred, axis=-1, keepdims=True) + EPS)
    normed = centred * inv_std
    return (normed, inv_std, normed * gain + bias)


def norm_back(upstream, normed, inv_std, gain):
    scaled = upstream * gain
    return inv_std * (
        scaled
        - jnp.mean(scaled, axis=-1, keepdims=True)
        - normed * jnp.mean(scaled * normed, axis=-1, keepdims=True)
    )


def gelu_parts(hidden_pre):
    cdf_value = 0.5 * (1.0 + jax.scipy.special.erf(hidden_pre * 2.0 ** (-0.5)))
    density = jnp.exp(-0.5 * hidden_pre * hidden_pre) * (2.0 * math.pi) ** (-0.5)
    return (hidden_pre * cdf_value, cdf_value + hidden_pre * density)


def contract_rows(left, right):
    return lax.dot_general(
        left, right, (((0,), (0,)), ((), ())), preferred_element_type=jnp.float32
    )


def contract_cols(left, right):
    return lax.dot_general(
        left, right, (((1,), (1,)), ((), ())), preferred_element_type=jnp.float32
    )


HEAD_COLS = 3 * HD
VMEM_BYTES = 48 << 20


def probs_of(packed, head, keep):
    start = head * HEAD_COLS
    query = packed[:, start : start + HD]
    key = packed[:, start + HD : start + 2 * HD]
    value = packed[:, start + 2 * HD : start + 3 * HD]
    scores = jnp.where(keep, contract_cols(key, query) * HD ** (-0.5), -1e30)
    powers = jnp.exp(scores - jnp.max(scores, axis=0, keepdims=True))
    probs = powers * (1.0 / jnp.sum(powers, axis=0, keepdims=True))
    return query, key, value, probs


def forward_kernel(
    tokens, gain, bias, weight, proj_bias, out_mine, out_theirs, low, packed, mixed, stats, mine,
    theirs,
):
    rows = tokens.shape[1]
    values = tokens[0].astype(jnp.float32)
    _, inv_std, scaled = layer_norm(values, gain[...], bias[...])
    first = lax.broadcasted_iota(jnp.int32, (rows, 128), 1) == 0
    stats[0] = jnp.where(first, jnp.mean(values, axis=-1, keepdims=True), inv_std)
    low[0] = scaled.astype(jnp.bfloat16)
    projected = jnp.dot(low[0], weight[...], preferred_element_type=jnp.float32)
    packed[0] = (projected + proj_bias[...]).astype(jnp.bfloat16)
    keep = lax.broadcasted_iota(jnp.int32, (rows, rows), 0) < TOK_IMG
    columns = packed[0]
    outs = []
    for head in range(weight.shape[1] // HEAD_COLS):
        _, _, value, probs = probs_of(columns, head, keep)
        outs.append(
            jnp.dot(
                value.astype(jnp.float32).T.astype(jnp.bfloat16),
                probs.astype(jnp.bfloat16),
                preferred_element_type=jnp.float32,
            )
        )
    mixed[0] = jnp.concatenate(outs, axis=0).T.astype(jnp.bfloat16)
    for part, out_weight in ((mine, out_mine), (theirs, out_theirs)):
        part[0] = jnp.dot(
            mixed[0], out_weight[...], preferred_element_type=jnp.float32
        ).astype(jnp.bfloat16)


def backward_kernel(
    core, tokens, attended_low, low2_mine, low2_theirs, cotangent, vectors, packed, out_weight,
    back_mine, back_theirs, residual_grad, upstream, grad, mine, theirs, query_sum, value_sum,
    feature_sums,
):
    rows = packed.shape[1]
    heads = packed.shape[2] // HEAD_COLS

    @pl.when(pl.program_id(0) == 0)
    def _():
        query_sum[...] = jnp.zeros_like(query_sum)
        value_sum[...] = jnp.zeros_like(value_sum)
        feature_sums[...] = jnp.zeros_like(feature_sums)

    attended = attended_low[0].astype(jnp.float32) + vectors[0:1]
    residual = tokens[0].astype(jnp.float32) + vectors[1:2] * attended
    normed, inv_std, _ = layer_norm(residual, vectors[2:3], vectors[3:4])
    grad_low2 = rejoin(core[0] == 1, low2_mine, low2_theirs)
    grad_residual = cotangent[0].astype(jnp.float32) + norm_back(
        grad_low2, normed, inv_std, vectors[2:3]
    )
    residual_grad[0] = grad_residual
    grad_attended = grad_residual * vectors[1:2]
    upstream[0] = grad_attended.astype(jnp.bfloat16)
    for row, product in enumerate(
        (grad_low2 * normed, grad_low2, grad_residual * attended, grad_attended)
    ):
        feature_sums[row : row + 1] += jnp.sum(product, axis=0, keepdims=True)
    grad_mixed = contract_cols(upstream[0], out_weight[...]).astype(jnp.bfloat16)
    keep = lax.broadcasted_iota(jnp.int32, (rows, rows), 0) < TOK_IMG
    columns = packed[0]
    queries = []
    for head in range(heads):
        query, key, value, probs = probs_of(columns, head, keep)
        grad_head = grad_mixed[:, head * HD : (head + 1) * HD]
        grad_probs = contract_cols(value, grad_head)
        delta = jnp.sum(probs * grad_probs, axis=0, keepdims=True)
        grad_scores = (probs * (grad_probs - delta) * HD ** (-0.5)).astype(jnp.bfloat16)
        grad_value = jnp.dot(
            probs.astype(jnp.bfloat16), grad_head, preferred_element_type=jnp.float32
        )
        grad_key = jnp.dot(grad_scores, query, preferred_element_type=jnp.float32)
        queries.append(
            jnp.dot(
                key.astype(jnp.float32).T.astype(jnp.bfloat16),
                grad_scores,
                preferred_element_type=jnp.float32,
            )
        )
        start = head * HEAD_COLS
        grad[0, :, start + HD : start + 2 * HD] = grad_key.astype(jnp.bfloat16)
        grad[0, :, start + 2 * HD : start + 3 * HD] = grad_value.astype(jnp.bfloat16)
        value_sum[:, head * HD : (head + 1) * HD] += jnp.sum(grad_value, axis=0, keepdims=True)
    grad_query = jnp.concatenate(queries, axis=0).T
    query_sum[...] += jnp.sum(grad_query, axis=0, keepdims=True)
    for head in range(heads):
        start = head * HEAD_COLS
        grad[0, :, start : start + HD] = grad_query[:, head * HD : (head + 1) * HD].astype(
            jnp.bfloat16
        )
    for part, weight in ((mine, back_mine), (theirs, back_theirs)):
        part[0] = contract_cols(grad[0], weight[...]).astype(jnp.bfloat16)


def rejoin(upper, mine, theirs):
    own, other = mine[0].astype(jnp.float32), theirs[0].astype(jnp.float32)
    return jnp.concatenate(
        [jnp.where(upper, other, own), jnp.where(upper, own, other)], axis=-1
    )


def hidden_kernel(
    core, tokens, mine, theirs, upstream, vectors, up_weight, up_bias, down_weight, up_mine,
    up_theirs, attended_low, low, activated_low, branch_grad, grad_low, part_mine, part_theirs,
    bias_sum,
):
    @pl.when(pl.program_id(0) == 0)
    def _():
        bias_sum[...] = jnp.zeros_like(bias_sum)

    joined = rejoin(core[0] == 1, mine, theirs)
    attended_low[0] = joined.astype(jnp.bfloat16)
    residual = tokens[0].astype(jnp.float32) + vectors[1:2] * (joined + vectors[0:1])
    _, _, scaled = layer_norm(residual, vectors[2:3], vectors[3:4])
    low[0] = scaled.astype(jnp.bfloat16)
    branch_grad[0] = (upstream[0].astype(jnp.float32) * vectors[4:5]).astype(jnp.bfloat16)
    hidden_pre = jnp.dot(low[0], up_weight[...], preferred_element_type=jnp.float32) + up_bias[...]
    activated, slope = gelu_parts(hidden_pre)
    activated_low[0] = activated.astype(jnp.bfloat16)
    grad_pre = contract_cols(branch_grad[0], down_weight[...]) * slope
    bias_sum[...] += jnp.sum(grad_pre, axis=0, keepdims=True)
    grad_low[0] = grad_pre.astype(jnp.bfloat16)
    for part, weight in ((part_mine, up_mine), (part_theirs, up_theirs)):
        part[0] = contract_cols(grad_low[0], weight[...]).astype(jnp.bfloat16)


def run_images(kernel, base, args, outs, name, core=None, carried=()):
    images, total = args[0].shape[0], max(out.shape[0] for out in outs if len(out.shape) == 3)

    def spec(shape):
        if len(shape) == 2:
            return pl.BlockSpec(shape, lambda image: (0, 0))
        first = base if shape[0] == total else 0
        return pl.BlockSpec((1,) + shape[1:], lambda image: (image + first, 0, 0))

    in_specs = [spec(arg.shape) for arg in args]
    if core is not None:
        in_specs = [pl.BlockSpec(memory_space=pltpu.SMEM)] + in_specs
        args = (core,) + tuple(args)
    skipped, count = len(carried), len(args)

    def body(*refs):
        kernel(*refs[:count], *refs[count + skipped :])

    return pl.pallas_call(
        body,
        grid=(images,),
        in_specs=in_specs + [pl.BlockSpec(memory_space=pl.ANY)] * skipped,
        out_specs=[spec(out.shape) for out in outs],
        out_shape=outs,
        input_output_aliases={count + index: index for index in range(skipped)},
        compiler_params=pltpu.CompilerParams(vmem_limit_bytes=VMEM_BYTES),
        name=name,
    )(*args, *carried)


def low_of(images, rows, width):
    return jax.ShapeDtypeStruct((images, rows, width), jnp.bfloat16)


def total_of(rows, width):
    return jax.ShapeDtypeStruct((rows, width), jnp.float32)


def attention_forward(total, base, carried, tokens, gain, bias, weight, *args):
    chunk, rows, features = tokens.shape
    out_mine = args[1]
    half = out_mine.shape[1]
    widths = (features, weight.shape[1], out_mine.shape[0])
    outs = [low_of(total, rows, width) for width in widths]
    outs += [jax.ShapeDtypeStruct((total, rows, 128), jnp.float32)]
    outs += [low_of(chunk, rows, half), low_of(chunk, rows, half)]
    args = (tokens, gain, bias, weight) + args
    return run_images(forward_kernel, base, args, outs, "attention_forward", None, carried)


def hidden_both(total, base, carried, core, tokens, mine, *args):
    chunk, rows, features = tokens.shape
    units, half = args[3].shape[1], mine.shape[2]
    widths = (features, features, units, features, units)
    outs = [low_of(total, rows, width) for width in widths]
    outs += [low_of(chunk, rows, half), low_of(chunk, rows, half), total_of(1, units)]
    args = (tokens, mine) + args
    return run_images(hidden_kernel, base, args, outs, "hidden_both", core, carried)


def attention_backward(total, base, carried, core, tokens, *args):
    chunk, rows, features = tokens.shape
    width, half = args[5].shape[2], args[7].shape[0]
    outs = [jax.ShapeDtypeStruct((total, rows, features), jnp.float32)]
    outs += [low_of(total, rows, columns) for columns in (features, width)]
    outs += [low_of(chunk, rows, half), low_of(chunk, rows, half)]
    outs += [total_of(1, width // 3), total_of(1, width // 3), total_of(4, features)]
    args = (tokens,) + args
    return run_images(backward_kernel, base, args, outs, "attention_backward", core, carried)


def exchange(block, axis, bit):
    size = lax.axis_size(axis)
    return lax.ppermute(block, axis, [(index, index ^ (1 << bit)) for index in range(size)])


def bit_of(axis, bit):
    return (lax.axis_index(axis) >> bit) % 2 == 1


def bits_in(axis):
    return (lax.axis_size(axis) - 1).bit_length()


def after(value, *others):
    return lax.optimization_barrier((value, *others))[0]


def split_blocks(values, dim):
    count = lax.axis_size("tensor")
    blocks = jnp.split(values, count, axis=dim)
    even = jnp.concatenate(blocks[0::2], axis=dim)
    odd = jnp.concatenate(blocks[1::2], axis=dim)
    upper = bit_of("tensor", 0)
    return jnp.where(upper, odd, even), jnp.where(upper, even, odd)


def split_halves(values, dim):
    low, high = jnp.split(values, 2, axis=dim)
    upper = bit_of("tensor", 0)
    return jnp.where(upper, high, low), jnp.where(upper, low, high)


def join_blocks(mine, theirs):
    count = lax.axis_size("tensor") // 2
    upper = bit_of("tensor", 0)
    pieces = []
    for own, other in zip(jnp.split(mine, count, axis=-1), jnp.split(theirs, count, axis=-1)):
        pieces += [jnp.where(upper, other, own), jnp.where(upper, own, other)]
    return jnp.concatenate(pieces, axis=-1)


def gather_far(block, others=()):
    for bit in range(1, bits_in("tensor")):
        got = after(exchange(block, "tensor", bit), others)
        upper = bit_of("tensor", bit)
        block = jnp.concatenate(
            [jnp.where(upper, got, block), jnp.where(upper, block, got)], axis=-1
        )
    return block


def gather_near(block):
    return join_blocks(block, exchange(block, "tensor", 0))


def add_near(mine, theirs, others=()):
    got = after(exchange(theirs, "tensor", 0), others)
    return (mine.astype(jnp.float32) + got.astype(jnp.float32)).astype(jnp.bfloat16)


def add_far(total, others=()):
    for bit in range(1, bits_in("tensor")):
        got = after(exchange(total, "tensor", bit), others)
        total = (total.astype(jnp.float32) + got.astype(jnp.float32)).astype(jnp.bfloat16)
    return total


def pick(terms, upper):
    halves = [jnp.split(term, 2, axis=0) for term in terms]
    return sum(jnp.where(upper, high, low).astype(jnp.float32) for low, high in halves)


def double_join(grad, got, bit):
    upper = bit_of("dp", bit)
    return jnp.concatenate([jnp.where(upper, got, grad), jnp.where(upper, grad, got)], axis=0)


def row_sums(name, flows):
    steps = len(flows[0][1])
    grads = [(grad, order) for group, order in flows for grad in group]
    orders = [order for _, order in grads]
    terms = [(grad,) for grad, _ in grads]
    for step in range(steps):
        uppers = [bit_of("dp", order[step]) for order in orders]
        sent = [
            pick(sums, jnp.logical_not(upper)).astype(jnp.bfloat16)
            for sums, upper in zip(terms, uppers)
        ]
        with jax.named_scope(f"{name}_halves_{step}"):
            got = [exchange(part, "dp", order[step]) for part, order in zip(sent, orders)]
        others = yield sent
        got = lax.optimization_barrier((got, others))[0]
        terms = [(pick(sums, upper), part) for sums, upper, part in zip(terms, uppers, got)]
    blocks = [sum(term.astype(jnp.float32) for term in sums) for sums in terms]
    blocks = [block.astype(jnp.bfloat16) for block in blocks]
    for step in reversed(range(steps)):
        with jax.named_scope(f"{name}_doubles_{step}"):
            got = [exchange(block, "dp", order[step]) for block, order in zip(blocks, orders)]
        others = yield blocks
        got = lax.optimization_barrier((got, others))[0]
        blocks = [
            double_join(block, part, order[step])
            for block, part, order in zip(blocks, got, orders)
        ]
    yield [block.astype(jnp.float32) for block in blocks]


def scatter_columns(results, name, parts):
    got = yield [exchange(theirs, "tensor", 0) for _, theirs in parts]
    totals = [
        flat(mine).astype(jnp.float32) + flat(part).astype(jnp.float32)
        for (mine, _), part in zip(parts, got)
    ]
    for bit in reversed(range(1, bits_in("tensor"))):
        upper = bit_of("tensor", bit)
        halves = [jnp.split(total, 2, axis=-1) for total in totals]
        got = yield [
            exchange(jnp.where(upper, low, high).astype(jnp.bfloat16), "tensor", bit)
            for low, high in halves
        ]
        totals = [
            jnp.where(upper, high, low) + part.astype(jnp.float32)
            for (low, high), part in zip(halves, got)
        ]
    results[name] = jnp.concatenate(totals, axis=0)


def sum_small(results, name, values, axis):
    sizes = [value.shape[0] for value in values]
    starts = [sum(sizes[:index]) for index in range(len(sizes))]
    packed = sum(
        jnp.pad(value, (start, sum(sizes) - start - size))
        for value, start, size in zip(values, starts, sizes)
    )
    for bit in range(bits_in(axis)):
        (got,) = yield [exchange(packed, axis, bit)]
        packed = packed + got
    sums, start = [], 0
    for value in values:
        sums.append(packed[start : start + value.shape[0]])
        start += value.shape[0]
    results[name] = sums


def gather_small(results, name, block):
    for bit in range(1, bits_in("tensor")):
        (got,) = yield [exchange(block, "tensor", bit)]
        upper = bit_of("tensor", bit)
        block = jnp.concatenate(
            [jnp.where(upper, got, block), jnp.where(upper, block, got)], axis=-1
        )
    (got,) = yield [exchange(block, "tensor", 0)]
    results[name] = join_blocks(block, got)


def flat(values):
    return values.reshape(-1, values.shape[-1])


class Tasks:
    def __init__(self):
        self.results, self.active = {}, []

    def add(self, task, name, *args):
        chain = task(self.results, name, *args)
        self.active.append((chain, next(chain)))

    def step(self, others):
        got = lax.optimization_barrier(([wanted for _, wanted in self.active], others))[0]
        chains, self.active = [chain for chain, _ in self.active], []
        for chain, arrived in zip(chains, got):
            try:
                self.active.append((chain, chain.send(arrived)))
            except StopIteration:
                pass
        return got


def shards(
    tokens,
    norm1_gain,
    norm1_bias,
    qkv_weight,
    query_bias,
    value_bias,
    out_weight,
    out_bias,
    layer_scale1,
    norm2_gain,
    norm2_bias,
    up_weight,
    up_bias,
    down_weight,
    down_bias,
    layer_scale2,
    cotangent,
):
    images = tokens.shape[0] // TOK_IMG
    width_local = tokens.shape[1]
    features = norm1_gain.shape[0]
    padded = -(-TOK_IMG // 8) * 8
    heads_local = query_bias.shape[0] // HD
    chunks = 2 if images % 2 == 0 else 1
    col_start = lax.axis_index("tensor") * width_local

    def cols(values):
        return lax.dynamic_slice_in_dim(values, col_start, width_local, values.ndim - 1)

    def pad_rows(values):
        values = values.reshape(images, TOK_IMG, width_local)
        return jnp.pad(values, ((0, 0), (0, padded - TOK_IMG), (0, 0)))

    def unpad_rows(values):
        values = values.reshape(images, padded, width_local)
        return values[:, :TOK_IMG].reshape(images * TOK_IMG, width_local)

    def in_chunks(values):
        return jnp.split(values, chunks, axis=0)

    def out_of_chunks(values):
        return jnp.concatenate(values, axis=0)

    count = images // chunks
    core = (lax.axis_index("tensor") % 2).astype(jnp.int32).reshape(1)
    proj_bias = jnp.stack(
        [
            query_bias.reshape(heads_local, HD),
            jnp.zeros((heads_local, HD), jnp.float32),
            value_bias.reshape(heads_local, HD),
        ],
        axis=1,
    ).reshape(1, 3 * heads_local * HD)
    tokens_given, cotangent_given = tokens, cotangent
    tokens = pad_rows(tokens)
    cotangent = pad_rows(cotangent)
    token_parts = in_chunks(tokens)
    out_mine, out_theirs = split_halves(out_weight, 1)
    up_mine, up_theirs = split_halves(up_weight, 0)
    qkv_mine, qkv_theirs = split_blocks(qkv_weight, 0)
    out_mine, out_theirs = after((out_mine, out_theirs), (up_mine, up_theirs, qkv_mine, qkv_theirs))
    far = gather_far(token_parts[0])
    later = lax.optimization_barrier((layer_scale2, token_parts[1:], cotangent, far))
    scale2_sent, token_parts[1:], cotangent_sent = later[:3]
    scale2_far = scale2_sent[None]
    whole, forward, carried, attended, sums, given = [], [], (), [], [], ()
    for index in range(chunks):
        joined = gather_near(far if index == 0 else gather_far(token_parts[index], given))
        whole.append(after(joined, attended))
        parts = attention_forward(
            images,
            index * count,
            carried,
            whole[index],
            norm1_gain[None],
            norm1_bias[None],
            qkv_weight,
            proj_bias,
            out_mine,
            out_theirs,
        )
        if index == 0:
            scale2_far = gather_far(scale2_far, parts[4])
            cotangent_far = gather_far(cotangent_sent)
        carried, given = parts[:4], parts[4:6]
        forward.append(parts)
        if index > 0:
            sums.append(add_far(attended[index - 1], given))
            given = after(given, sums[-1])
        attended.append(add_near(*given))
    packed = carried[1]
    lowered1, mixed, stats1 = flat(carried[0]), flat(carried[2]), flat(carried[3])
    scale2_far = after(scale2_far, attended)
    upstream = in_chunks(gather_near(after(cotangent_far, attended)))
    scale2_all = gather_near(scale2_far)
    vectors = jnp.concatenate(
        [out_bias[None], layer_scale1[None], norm2_gain[None], norm2_bias[None], scale2_all]
    )

    hidden, carried, low2, given = [], (), [], (vectors, upstream)
    for index in range(chunks):
        if index == chunks - 1:
            sums.append(add_far(attended[index], given))
        mine = sums[index]
        theirs = exchange(mine, "tensor", 0)
        parts = hidden_both(
            images,
            index * count,
            carried,
            core,
            whole[index],
            after(mine, low2),
            theirs,
            upstream[index],
            vectors,
            up_weight,
            up_bias[None],
            down_weight,
            up_mine,
            up_theirs,
        )
        carried, given = parts[:5], parts[5:7]
        hidden.append(parts)
        if index < chunks - 1:
            low2.append(add_near(*given))
    attended_low = carried[0]
    lowered2, activated_low, branch_grad, grad_pre_low = (flat(part) for part in carried[1:])
    grad_up_bias = sum(parts[7] for parts in hidden)[0]
    grad_down_weight = contract_rows(activated_low, branch_grad)
    low2.append(add_near(*given, grad_down_weight))
    low2_sums = [add_far(low2[0], low2[-1:])]
    low2_theirs = [exchange(low2_sums[0], "tensor", 0)]
    grad_up_weight = contract_rows(after(lowered2, low2_sums), grad_pre_low)
    first_order = tuple(range(bits_in("dp")))
    second_order = first_order[1:2] + first_order[:1] + first_order[2:]
    hidden_sums = row_sums(
        "hidden", [([grad_down_weight], first_order), ([grad_up_weight], second_order)]
    )
    sent = next(hidden_sums)

    tasks = Tasks()
    results = tasks.results
    back, carried, given = [], (), sent
    for index in range(chunks):
        if index == chunks - 1:
            activated_late, *down_late = after((activated_low, *split_blocks(down_weight, 1)), given)
            branch_parts = [
                jnp.dot(activated_late, weight, preferred_element_type=jnp.float32).astype(
                    jnp.bfloat16
                )
                for weight in down_late
            ]
            tasks.add(scatter_columns, "branch", [branch_parts])
            given = branch_parts
        if index > 0:
            low2_sums.append(add_far(low2[index], given))
            low2_theirs.append(exchange(low2_sums[index], "tensor", 0))
        mine, theirs = after((low2_sums[index], low2_theirs[index]), given)
        parts = attention_backward(
            images,
            index * count,
            carried,
            core,
            whole[index],
            attended_low,
            mine,
            theirs,
            upstream[index],
            vectors,
            packed,
            out_weight,
            qkv_mine,
            qkv_theirs,
        )
        carried, given = parts[:3], parts[3:5]
        back.append(parts)
    residual_grad, grad_attended, grad_projected = (flat(part) for part in carried)
    tasks.add(scatter_columns, "lowered1", [parts[3:5] for parts in back])
    state = hidden_sums.send(given)
    late = after(
        (tokens_given, cotangent_given, norm1_gain, layer_scale1, out_bias), state
    )
    tokens_late, cotangent_late, gain1_late, scale1_late, out_bias_late = late
    grad_attended, grad_projected = after((grad_attended, grad_projected), state)
    grad_out_weight = contract_rows(mixed, grad_attended)
    grad_qkv_weight = contract_rows(lowered1, grad_projected)
    state = hidden_sums.send((grad_out_weight, grad_qkv_weight))
    rows = grad_qkv_weight.shape[0]
    first_rows = 3 * rows // 8
    grad_out_weight, grad_qkv_weight = after((grad_out_weight, grad_qkv_weight), state)
    heads_sums = row_sums(
        "heads",
        [
            ([grad_out_weight, grad_qkv_weight[:first_rows]], first_order),
            ([grad_qkv_weight[first_rows:]], second_order),
        ],
    )
    last = next(heads_sums)

    def finish(others):
        if "branch" in results and "output" not in results:
            branch_cols = results["branch"] + down_bias
            own, upstream_own = flat(pad_rows(tokens_late)), flat(pad_rows(cotangent_late))
            attended_cols = cols(flat(attended_low)).astype(jnp.float32) + cols(out_bias_late)
            residual_cols = own.astype(jnp.float32) + cols(scale1_late) * attended_cols
            results["output"] = unpad_rows(residual_cols + layer_scale2 * branch_cols)
            upstream_cols = upstream_own.astype(jnp.float32)
            results["scale2"] = jnp.sum(upstream_cols * branch_cols, axis=0)
            results["down_bias"] = jnp.sum(upstream_cols * layer_scale2, axis=0)
        if "lowered1" in results and "scaled" not in results:
            grad_lowered1 = results["lowered1"]
            row_mean, inv_std1 = stats1[:, 0:1], stats1[:, 1:2]
            normed1 = (flat(pad_rows(tokens_late)).astype(jnp.float32) - row_mean) * inv_std1
            scaled = grad_lowered1 * cols(gain1_late)
            results["scaled"] = (scaled, normed1, inv_std1)
            tasks.add(
                sum_small,
                "row_totals",
                [jnp.sum(scaled, axis=-1), jnp.sum(scaled * normed1, axis=-1)],
                "tensor",
            )
            results["norm1"] = [
                jnp.sum(grad_lowered1 * normed1, axis=0),
                jnp.sum(grad_lowered1, axis=0),
            ]
        if "norm1" in results and "output" in results and "packed" not in results:
            feature_sums = sum(parts[7] for parts in back)
            results["packed"] = [
                sum(parts[5] for parts in back)[0],
                sum(parts[6] for parts in back)[0],
                feature_sums[3],
                feature_sums[2],
                feature_sums[0],
                feature_sums[1],
                grad_up_bias,
                results["down_bias"],
                results["scale2"],
            ] + results["norm1"]
            tasks.add(sum_small, "small", results["packed"], "dp")
        if "row_totals" in results and "input_grad" not in results:
            scaled, normed1, inv_std1 = results["scaled"]
            mean_scaled, mean_product = (
                values[:, None] / features for values in results["row_totals"]
            )
            results["input_grad"] = unpad_rows(
                cols(residual_grad) + inv_std1 * (scaled - mean_scaled - normed1 * mean_product)
            )
        if "small" in results and "norm1_sums" not in results:
            results["norm1_sums"] = None
            tasks.add(gather_small, "norm1_all", jnp.stack(results["small"][9:]))

    finished = {}
    last = tasks.step((state, last))
    finish(last)
    for step in range(2 * len(first_order)):
        if step < 2 * len(first_order) - 2:
            finished["hidden"] = hidden_sums.send(last)
        finished["heads"] = heads_sums.send(last)
        last = list(finished.values())
        if tasks.active:
            last = (last, tasks.step(last))
            finish(last)
    while tasks.active:
        last = tasks.step(last)
        finish(last)
    grad_down_weight, grad_up_weight = finished["hidden"]
    grad_out_weight, top, bottom = finished["heads"]
    grad_qkv_weight = jnp.concatenate([top, bottom], axis=0)
    (
        grad_query_bias,
        grad_value_bias,
        grad_out_bias,
        grad_layer_scale1,
        grad_norm2_gain,
        grad_norm2_bias,
        grad_up_bias,
        grad_down_bias,
        grad_layer_scale2,
    ) = results["small"][:9]
    grad_norm1_gain, grad_norm1_bias = results["norm1_all"]
    output, input_grad = results["output"], results["input_grad"]
    return (
        output,
        input_grad,
        grad_norm1_gain,
        grad_norm1_bias,
        grad_qkv_weight,
        grad_query_bias,
        grad_value_bias,
        grad_out_weight,
        grad_out_bias,
        grad_layer_scale1,
        grad_norm2_gain,
        grad_norm2_bias,
        grad_up_weight,
        grad_up_bias,
        grad_down_weight,
        grad_down_bias,
        grad_layer_scale2,
    )


def solution(mesh):
    return jax.shard_map(
        shards,
        mesh=mesh,
        in_specs=(
            P("dp", "tensor"),
            P(),
            P(),
            P(None, "tensor"),
            P("tensor"),
            P("tensor"),
            P("tensor", None),
            P(),
            P(),
            P(),
            P(),
            P(None, "tensor"),
            P("tensor"),
            P("tensor", None),
            P("tensor"),
            P("tensor"),
            P("dp", "tensor"),
        ),
        out_specs=(
            P("dp", "tensor"),
            P("dp", "tensor"),
            P(),
            P(),
            P(None, "tensor"),
            P("tensor"),
            P("tensor"),
            P("tensor", None),
            P(),
            P(),
            P(),
            P(),
            P(None, "tensor"),
            P("tensor"),
            P("tensor", None),
            P("tensor"),
            P("tensor"),
        ),
        check_vma=False,
    )
```

```python
import math

import jax
import jax.numpy as jnp
from jax import lax
from jax.experimental import pallas as pl
from jax.experimental.pallas import tpu as pltpu
from jax.sharding import PartitionSpec as P

HD = 64
TOK_IMG = 257


EPS = 1e-06


def layer_norm(values, gain, bias):
    row_mean = jnp.mean(values, axis=-1, keepdims=True)
    centred = values - row_mean
    inv_std = lax.rsqrt(jnp.mean(centred * centred, axis=-1, keepdims=True) + EPS)
    normed = centred * inv_std
    return (normed, inv_std, normed * gain + bias)


def norm_back(upstream, normed, inv_std, gain):
    scaled = upstream * gain
    return inv_std * (
        scaled
        - jnp.mean(scaled, axis=-1, keepdims=True)
        - normed * jnp.mean(scaled * normed, axis=-1, keepdims=True)
    )


def gelu_parts(hidden_pre):
    cdf_value = 0.5 * (1.0 + jax.scipy.special.erf(hidden_pre * 2.0 ** (-0.5)))
    density = jnp.exp(-0.5 * hidden_pre * hidden_pre) * (2.0 * math.pi) ** (-0.5)
    return (hidden_pre * cdf_value, cdf_value + hidden_pre * density)


def contract_rows(left, right):
    return lax.dot_general(
        left, right, (((0,), (0,)), ((), ())), preferred_element_type=jnp.float32
    )


def contract_cols(left, right):
    return lax.dot_general(
        left, right, (((1,), (1,)), ((), ())), preferred_element_type=jnp.float32
    )


HEAD_COLS = 3 * HD
VMEM_BYTES = 48 << 20


def probs_of(packed, head, keep):
    start = head * HEAD_COLS
    query = packed[:, start : start + HD]
    key = packed[:, start + HD : start + 2 * HD]
    value = packed[:, start + 2 * HD : start + 3 * HD]
    scores = jnp.where(keep, contract_cols(key, query) * HD ** (-0.5), -1e30)
    powers = jnp.exp(scores - jnp.max(scores, axis=0, keepdims=True))
    probs = powers * (1.0 / jnp.sum(powers, axis=0, keepdims=True))
    return query, key, value, probs


def forward_kernel(
    tokens, gain, bias, weight, proj_bias, out_mine, out_theirs, low, packed, mixed, stats, mine,
    theirs,
):
    rows = tokens.shape[1]
    values = tokens[0].astype(jnp.float32)
    _, inv_std, scaled = layer_norm(values, gain[...], bias[...])
    first = lax.broadcasted_iota(jnp.int32, (rows, 128), 1) == 0
    stats[0] = jnp.where(first, jnp.mean(values, axis=-1, keepdims=True), inv_std)
    low[0] = scaled.astype(jnp.bfloat16)
    projected = jnp.dot(low[0], weight[...], preferred_element_type=jnp.float32)
    packed[0] = (projected + proj_bias[...]).astype(jnp.bfloat16)
    keep = lax.broadcasted_iota(jnp.int32, (rows, rows), 0) < TOK_IMG
    columns = packed[0]
    outs = []
    for head in range(weight.shape[1] // HEAD_COLS):
        _, _, value, probs = probs_of(columns, head, keep)
        outs.append(
            jnp.dot(
                value.astype(jnp.float32).T.astype(jnp.bfloat16),
                probs.astype(jnp.bfloat16),
                preferred_element_type=jnp.float32,
            )
        )
    mixed[0] = jnp.concatenate(outs, axis=0).T.astype(jnp.bfloat16)
    for part, out_weight in ((mine, out_mine), (theirs, out_theirs)):
        part[0] = jnp.dot(
            mixed[0], out_weight[...], preferred_element_type=jnp.float32
        ).astype(jnp.bfloat16)


def backward_kernel(
    core, tokens, attended_low, low2_mine, low2_theirs, cotangent, vectors, packed, out_weight,
    back_mine, back_theirs, residual_grad, upstream, grad, mine, theirs, query_sum, value_sum,
    feature_sums,
):
    rows = packed.shape[1]
    heads = packed.shape[2] // HEAD_COLS

    @pl.when(pl.program_id(0) == 0)
    def _():
        query_sum[...] = jnp.zeros_like(query_sum)
        value_sum[...] = jnp.zeros_like(value_sum)
        feature_sums[...] = jnp.zeros_like(feature_sums)

    attended = attended_low[0].astype(jnp.float32) + vectors[0:1]
    residual = tokens[0].astype(jnp.float32) + vectors[1:2] * attended
    normed, inv_std, _ = layer_norm(residual, vectors[2:3], vectors[3:4])
    grad_low2 = rejoin(core[0] == 1, low2_mine, low2_theirs)
    grad_residual = cotangent[0].astype(jnp.float32) + norm_back(
        grad_low2, normed, inv_std, vectors[2:3]
    )
    residual_grad[0] = grad_residual
    grad_attended = grad_residual * vectors[1:2]
    upstream[0] = grad_attended.astype(jnp.bfloat16)
    for row, product in enumerate(
        (grad_low2 * normed, grad_low2, grad_residual * attended, grad_attended)
    ):
        feature_sums[row : row + 1] += jnp.sum(product, axis=0, keepdims=True)
    grad_mixed = contract_cols(upstream[0], out_weight[...]).astype(jnp.bfloat16)
    keep = lax.broadcasted_iota(jnp.int32, (rows, rows), 0) < TOK_IMG
    columns = packed[0]
    queries = []
    for head in range(heads):
        query, key, value, probs = probs_of(columns, head, keep)
        grad_head = grad_mixed[:, head * HD : (head + 1) * HD]
        grad_probs = contract_cols(value, grad_head)
        delta = jnp.sum(probs * grad_probs, axis=0, keepdims=True)
        grad_scores = (probs * (grad_probs - delta) * HD ** (-0.5)).astype(jnp.bfloat16)
        grad_value = jnp.dot(
            probs.astype(jnp.bfloat16), grad_head, preferred_element_type=jnp.float32
        )
        grad_key = jnp.dot(grad_scores, query, preferred_element_type=jnp.float32)
        queries.append(
            jnp.dot(
                key.astype(jnp.float32).T.astype(jnp.bfloat16),
                grad_scores,
                preferred_element_type=jnp.float32,
            )
        )
        start = head * HEAD_COLS
        grad[0, :, start + HD : start + 2 * HD] = grad_key.astype(jnp.bfloat16)
        grad[0, :, start + 2 * HD : start + 3 * HD] = grad_value.astype(jnp.bfloat16)
        value_sum[:, head * HD : (head + 1) * HD] += jnp.sum(grad_value, axis=0, keepdims=True)
    grad_query = jnp.concatenate(queries, axis=0).T
    query_sum[...] += jnp.sum(grad_query, axis=0, keepdims=True)
    for head in range(heads):
        start = head * HEAD_COLS
        grad[0, :, start : start + HD] = grad_query[:, head * HD : (head + 1) * HD].astype(
            jnp.bfloat16
        )
    for part, weight in ((mine, back_mine), (theirs, back_theirs)):
        part[0] = contract_cols(grad[0], weight[...]).astype(jnp.bfloat16)


def rejoin(upper, mine, theirs):
    own, other = mine[0].astype(jnp.float32), theirs[0].astype(jnp.float32)
    return jnp.concatenate(
        [jnp.where(upper, other, own), jnp.where(upper, own, other)], axis=-1
    )


def hidden_kernel(
    core, tokens, mine, theirs, upstream, vectors, up_weight, up_bias, down_weight, up_mine,
    up_theirs, attended_low, low, activated_low, branch_grad, grad_low, part_mine, part_theirs,
    bias_sum,
):
    @pl.when(pl.program_id(0) == 0)
    def _():
        bias_sum[...] = jnp.zeros_like(bias_sum)

    joined = rejoin(core[0] == 1, mine, theirs)
    attended_low[0] = joined.astype(jnp.bfloat16)
    residual = tokens[0].astype(jnp.float32) + vectors[1:2] * (joined + vectors[0:1])
    _, _, scaled = layer_norm(residual, vectors[2:3], vectors[3:4])
    low[0] = scaled.astype(jnp.bfloat16)
    branch_grad[0] = (upstream[0].astype(jnp.float32) * vectors[4:5]).astype(jnp.bfloat16)
    hidden_pre = jnp.dot(low[0], up_weight[...], preferred_element_type=jnp.float32) + up_bias[...]
    activated, slope = gelu_parts(hidden_pre)
    activated_low[0] = activated.astype(jnp.bfloat16)
    grad_pre = contract_cols(branch_grad[0], down_weight[...]) * slope
    bias_sum[...] += jnp.sum(grad_pre, axis=0, keepdims=True)
    grad_low[0] = grad_pre.astype(jnp.bfloat16)
    for part, weight in ((part_mine, up_mine), (part_theirs, up_theirs)):
        part[0] = contract_cols(grad_low[0], weight[...]).astype(jnp.bfloat16)


def run_images(kernel, base, args, outs, name, core=None, carried=()):
    images, total = args[0].shape[0], max(out.shape[0] for out in outs if len(out.shape) == 3)

    def spec(shape):
        if len(shape) == 2:
            return pl.BlockSpec(shape, lambda image: (0, 0))
        first = base if shape[0] == total else 0
        return pl.BlockSpec((1,) + shape[1:], lambda image: (image + first, 0, 0))

    in_specs = [spec(arg.shape) for arg in args]
    if core is not None:
        in_specs = [pl.BlockSpec(memory_space=pltpu.SMEM)] + in_specs
        args = (core,) + tuple(args)
    skipped, count = len(carried), len(args)

    def body(*refs):
        kernel(*refs[:count], *refs[count + skipped :])

    return pl.pallas_call(
        body,
        grid=(images,),
        in_specs=in_specs + [pl.BlockSpec(memory_space=pl.ANY)] * skipped,
        out_specs=[spec(out.shape) for out in outs],
        out_shape=outs,
        input_output_aliases={count + index: index for index in range(skipped)},
        compiler_params=pltpu.CompilerParams(vmem_limit_bytes=VMEM_BYTES),
        name=name,
    )(*args, *carried)


def low_of(images, rows, width):
    return jax.ShapeDtypeStruct((images, rows, width), jnp.bfloat16)


def total_of(rows, width):
    return jax.ShapeDtypeStruct((rows, width), jnp.float32)


def attention_forward(total, base, carried, tokens, gain, bias, weight, *args):
    chunk, rows, features = tokens.shape
    out_mine = args[1]
    half = out_mine.shape[1]
    widths = (features, weight.shape[1], out_mine.shape[0])
    outs = [low_of(total, rows, width) for width in widths]
    outs += [jax.ShapeDtypeStruct((total, rows, 128), jnp.float32)]
    outs += [low_of(chunk, rows, half), low_of(chunk, rows, half)]
    args = (tokens, gain, bias, weight) + args
    return run_images(forward_kernel, base, args, outs, "attention_forward", None, carried)


def hidden_both(total, base, carried, core, tokens, mine, *args):
    chunk, rows, features = tokens.shape
    units, half = args[3].shape[1], mine.shape[2]
    widths = (features, features, units, features, units)
    outs = [low_of(total, rows, width) for width in widths]
    outs += [low_of(chunk, rows, half), low_of(chunk, rows, half), total_of(1, units)]
    args = (tokens, mine) + args
    return run_images(hidden_kernel, base, args, outs, "hidden_both", core, carried)


def attention_backward(total, base, carried, core, tokens, *args):
    chunk, rows, features = tokens.shape
    width, half = args[5].shape[2], args[7].shape[0]
    outs = [jax.ShapeDtypeStruct((total, rows, features), jnp.float32)]
    outs += [low_of(total, rows, columns) for columns in (features, width)]
    outs += [low_of(chunk, rows, half), low_of(chunk, rows, half)]
    outs += [total_of(1, width // 3), total_of(1, width // 3), total_of(4, features)]
    args = (tokens,) + args
    return run_images(backward_kernel, base, args, outs, "attention_backward", core, carried)


def exchange(block, axis, bit):
    size = lax.axis_size(axis)
    return lax.ppermute(block, axis, [(index, index ^ (1 << bit)) for index in range(size)])


def bit_of(axis, bit):
    return (lax.axis_index(axis) >> bit) % 2 == 1


def bits_in(axis):
    return (lax.axis_size(axis) - 1).bit_length()


def after(value, *others):
    return lax.optimization_barrier((value, *others))[0]


def split_blocks(values, dim):
    count = lax.axis_size("tensor")
    blocks = jnp.split(values, count, axis=dim)
    even = jnp.concatenate(blocks[0::2], axis=dim)
    odd = jnp.concatenate(blocks[1::2], axis=dim)
    upper = bit_of("tensor", 0)
    return jnp.where(upper, odd, even), jnp.where(upper, even, odd)


def split_halves(values, dim):
    low, high = jnp.split(values, 2, axis=dim)
    upper = bit_of("tensor", 0)
    return jnp.where(upper, high, low), jnp.where(upper, low, high)


def join_blocks(mine, theirs):
    count = lax.axis_size("tensor") // 2
    upper = bit_of("tensor", 0)
    pieces = []
    for own, other in zip(jnp.split(mine, count, axis=-1), jnp.split(theirs, count, axis=-1)):
        pieces += [jnp.where(upper, other, own), jnp.where(upper, own, other)]
    return jnp.concatenate(pieces, axis=-1)


def gather_far(block, others=()):
    for bit in range(1, bits_in("tensor")):
        got = after(exchange(block, "tensor", bit), others)
        upper = bit_of("tensor", bit)
        block = jnp.concatenate(
            [jnp.where(upper, got, block), jnp.where(upper, block, got)], axis=-1
        )
    return block


def gather_near(block):
    return join_blocks(block, exchange(block, "tensor", 0))


def add_near(mine, theirs, others=()):
    got = after(exchange(theirs, "tensor", 0), others)
    return (mine.astype(jnp.float32) + got.astype(jnp.float32)).astype(jnp.bfloat16)


def add_far(total, others=()):
    for bit in range(1, bits_in("tensor")):
        got = after(exchange(total, "tensor", bit), others)
        total = (total.astype(jnp.float32) + got.astype(jnp.float32)).astype(jnp.bfloat16)
    return total


def pick(terms, upper):
    halves = [jnp.split(term, 2, axis=0) for term in terms]
    return sum(jnp.where(upper, high, low).astype(jnp.float32) for low, high in halves)


def double_join(grad, got, bit):
    upper = bit_of("dp", bit)
    return jnp.concatenate([jnp.where(upper, got, grad), jnp.where(upper, grad, got)], axis=0)


def row_sums(name, flows):
    steps = len(flows[0][1])
    grads = [(grad, order) for group, order in flows for grad in group]
    orders = [order for _, order in grads]
    terms = [(grad,) for grad, _ in grads]
    for step in range(steps):
        uppers = [bit_of("dp", order[step]) for order in orders]
        sent = [
            pick(sums, jnp.logical_not(upper)).astype(jnp.bfloat16)
            for sums, upper in zip(terms, uppers)
        ]
        with jax.named_scope(f"{name}_halves_{step}"):
            got = [exchange(part, "dp", order[step]) for part, order in zip(sent, orders)]
        others = yield sent
        got = lax.optimization_barrier((got, others))[0]
        terms = [(pick(sums, upper), part) for sums, upper, part in zip(terms, uppers, got)]
    blocks = [sum(term.astype(jnp.float32) for term in sums) for sums in terms]
    blocks = [block.astype(jnp.bfloat16) for block in blocks]
    for step in reversed(range(steps)):
        with jax.named_scope(f"{name}_doubles_{step}"):
            got = [exchange(block, "dp", order[step]) for block, order in zip(blocks, orders)]
        others = yield blocks
        got = lax.optimization_barrier((got, others))[0]
        blocks = [
            double_join(block, part, order[step])
            for block, part, order in zip(blocks, got, orders)
        ]
    yield [block.astype(jnp.float32) for block in blocks]


def scatter_columns(results, name, parts):
    got = yield [exchange(theirs, "tensor", 0) for _, theirs in parts]
    totals = [
        flat(mine).astype(jnp.float32) + flat(part).astype(jnp.float32)
        for (mine, _), part in zip(parts, got)
    ]
    for bit in reversed(range(1, bits_in("tensor"))):
        upper = bit_of("tensor", bit)
        halves = [jnp.split(total, 2, axis=-1) for total in totals]
        got = yield [
            exchange(jnp.where(upper, low, high).astype(jnp.bfloat16), "tensor", bit)
            for low, high in halves
        ]
        totals = [
            jnp.where(upper, high, low) + part.astype(jnp.float32)
            for (low, high), part in zip(halves, got)
        ]
    results[name] = jnp.concatenate(totals, axis=0)


def sum_small(results, name, values, axis):
    sizes = [value.shape[0] for value in values]
    starts = [sum(sizes[:index]) for index in range(len(sizes))]
    packed = sum(
        jnp.pad(value, (start, sum(sizes) - start - size))
        for value, start, size in zip(values, starts, sizes)
    )
    for bit in range(bits_in(axis)):
        (got,) = yield [exchange(packed, axis, bit)]
        packed = packed + got
    sums, start = [], 0
    for value in values:
        sums.append(packed[start : start + value.shape[0]])
        start += value.shape[0]
    results[name] = sums


def gather_small(results, name, block):
    for bit in range(1, bits_in("tensor")):
        (got,) = yield [exchange(block, "tensor", bit)]
        upper = bit_of("tensor", bit)
        block = jnp.concatenate(
            [jnp.where(upper, got, block), jnp.where(upper, block, got)], axis=-1
        )
    (got,) = yield [exchange(block, "tensor", 0)]
    results[name] = join_blocks(block, got)


def flat(values):
    return values.reshape(-1, values.shape[-1])


class Tasks:
    def __init__(self):
        self.results, self.active = {}, []

    def add(self, task, name, *args):
        chain = task(self.results, name, *args)
        self.active.append((chain, next(chain)))

    def step(self, others):
        got = lax.optimization_barrier(([wanted for _, wanted in self.active], others))[0]
        chains, self.active = [chain for chain, _ in self.active], []
        for chain, arrived in zip(chains, got):
            try:
                self.active.append((chain, chain.send(arrived)))
            except StopIteration:
                pass
        return got


def shards(
    tokens,
    norm1_gain,
    norm1_bias,
    qkv_weight,
    query_bias,
    value_bias,
    out_weight,
    out_bias,
    layer_scale1,
    norm2_gain,
    norm2_bias,
    up_weight,
    up_bias,
    down_weight,
    down_bias,
    layer_scale2,
    cotangent,
):
    images = tokens.shape[0] // TOK_IMG
    width_local = tokens.shape[1]
    features = norm1_gain.shape[0]
    padded = -(-TOK_IMG // 8) * 8
    heads_local = query_bias.shape[0] // HD
    chunks = 2 if images % 2 == 0 else 1
    col_start = lax.axis_index("tensor") * width_local

    def cols(values):
        return lax.dynamic_slice_in_dim(values, col_start, width_local, values.ndim - 1)

    def pad_rows(values):
        values = values.reshape(images, TOK_IMG, width_local)
        return jnp.pad(values, ((0, 0), (0, padded - TOK_IMG), (0, 0)))

    def unpad_rows(values):
        values = values.reshape(images, padded, width_local)
        return values[:, :TOK_IMG].reshape(images * TOK_IMG, width_local)

    def in_chunks(values):
        return jnp.split(values, chunks, axis=0)

    def out_of_chunks(values):
        return jnp.concatenate(values, axis=0)

    count = images // chunks
    core = (lax.axis_index("tensor") % 2).astype(jnp.int32).reshape(1)
    proj_bias = jnp.stack(
        [
            query_bias.reshape(heads_local, HD),
            jnp.zeros((heads_local, HD), jnp.float32),
            value_bias.reshape(heads_local, HD),
        ],
        axis=1,
    ).reshape(1, 3 * heads_local * HD)
    tokens_given, cotangent_given = tokens, cotangent
    tokens = pad_rows(tokens)
    cotangent = pad_rows(cotangent)
    token_parts = in_chunks(tokens)
    out_mine, out_theirs = split_halves(out_weight, 1)
    up_mine, up_theirs = split_halves(up_weight, 0)
    qkv_mine, qkv_theirs = split_blocks(qkv_weight, 0)
    out_mine, out_theirs = after((out_mine, out_theirs), (up_mine, up_theirs, qkv_mine, qkv_theirs))
    far = gather_far(token_parts[0])
    scale2_sent, rest_sent = after(
        (layer_scale2, jnp.concatenate(token_parts[1:] + [cotangent], axis=0)), far
    )
    scale2_far = scale2_sent[None]
    whole, forward, carried, attended, sums, given = [], [], (), [], [], ()
    for index in range(chunks):
        joined = gather_near(far if index == 0 else rest_far[(index - 1) * count : index * count])
        whole.append(after(joined, attended))
        parts = attention_forward(
            images,
            index * count,
            carried,
            whole[index],
            norm1_gain[None],
            norm1_bias[None],
            qkv_weight,
            proj_bias,
            out_mine,
            out_theirs,
        )
        if index == 0:
            scale2_far = gather_far(scale2_far, parts[4])
            rest_far = gather_far(rest_sent, parts[4:6])
            cotangent_far = rest_far[images - count :]
        carried, given = parts[:4], parts[4:6]
        forward.append(parts)
        if index > 0:
            sums.append(add_far(attended[index - 1], given))
            given = after(given, sums[-1])
        attended.append(add_near(*given))
    packed = carried[1]
    lowered1, mixed, stats1 = flat(carried[0]), flat(carried[2]), flat(carried[3])
    scale2_far = after(scale2_far, forward[-1][4])
    upstream = gather_near(after(cotangent_far, forward[-1][4]))
    scale2_all = gather_near(scale2_far)
    vectors = jnp.concatenate(
        [out_bias[None], layer_scale1[None], norm2_gain[None], norm2_bias[None], scale2_all]
    )

    hidden, carried, low2, given = [], (), [], (vectors, upstream)
    for index in range(chunks):
        if index == chunks - 1:
            sums.append(add_far(attended[index], given))
        mine = sums[index]
        theirs = exchange(mine, "tensor", 0)
        parts = hidden_both(
            images,
            index * count,
            carried,
            core,
            whole[index],
            after(mine, low2),
            theirs,
            upstream,
            vectors,
            up_weight,
            up_bias[None],
            down_weight,
            up_mine,
            up_theirs,
        )
        carried, given = parts[:5], parts[5:7]
        hidden.append(parts)
        if index < chunks - 1:
            low2.append(add_near(*given))
    attended_low = carried[0]
    lowered2, activated_low, branch_grad, grad_pre_low = (flat(part) for part in carried[1:])
    grad_up_bias = sum(parts[7] for parts in hidden)[0]
    grad_down_weight = contract_rows(activated_low, branch_grad)
    low2.append(add_near(*given, grad_down_weight))
    low2_sums = [add_far(low2[0], low2[-1:])]
    low2_theirs = [exchange(low2_sums[0], "tensor", 0)]
    grad_up_weight = contract_rows(after(lowered2, low2_sums), grad_pre_low)
    first_order = tuple(range(bits_in("dp")))
    second_order = first_order[1:2] + first_order[:1] + first_order[2:]
    hidden_sums = row_sums(
        "hidden", [([grad_down_weight], first_order), ([grad_up_weight], second_order)]
    )
    sent = next(hidden_sums)

    tasks = Tasks()
    results = tasks.results
    back, carried, given = [], (), sent
    for index in range(chunks):
        if index > 0:
            low2_sums.append(add_far(low2[index], given))
            low2_theirs.append(exchange(low2_sums[index], "tensor", 0))
        mine, theirs = after((low2_sums[index], low2_theirs[index]), given)
        parts = attention_backward(
            images,
            index * count,
            carried,
            core,
            whole[index],
            attended_low,
            mine,
            theirs,
            upstream,
            vectors,
            packed,
            out_weight,
            qkv_mine,
            qkv_theirs,
        )
        carried, given = parts[:3], parts[3:5]
        back.append(parts)
        tasks.add(scatter_columns, index, [given])
    residual_grad, grad_attended, grad_projected = (flat(part) for part in carried)
    state = hidden_sums.send(given)
    state = (state, tasks.step(state))
    grad_attended, grad_projected = after((grad_attended, grad_projected), state)
    grad_out_weight = contract_rows(mixed, grad_attended)
    grad_qkv_weight = contract_rows(lowered1, grad_projected)
    state = hidden_sums.send((grad_out_weight, grad_qkv_weight))
    rows = grad_qkv_weight.shape[0]
    first_rows = 3 * rows // 8
    grad_out_weight, grad_qkv_weight = after((grad_out_weight, grad_qkv_weight), state)
    heads_sums = row_sums(
        "heads",
        [
            ([grad_out_weight, grad_qkv_weight[:first_rows]], first_order),
            ([grad_qkv_weight[first_rows:]], second_order),
        ],
    )
    last = next(heads_sums)
    late = after(
        (tokens_given, cotangent_given, norm1_gain, layer_scale1, out_bias, activated_low), last
    )
    tokens_late, cotangent_late, gain1_late, scale1_late, out_bias_late, activated_late = late
    def finish(others):
        if "branch" in results and "output" not in results:
            branch_cols = results["branch"] + down_bias
            own, upstream_own = flat(pad_rows(tokens_late)), flat(pad_rows(cotangent_late))
            attended_cols = cols(flat(attended_low)).astype(jnp.float32) + cols(out_bias_late)
            residual_cols = own.astype(jnp.float32) + cols(scale1_late) * attended_cols
            results["output"] = unpad_rows(residual_cols + layer_scale2 * branch_cols)
            upstream_cols = upstream_own.astype(jnp.float32)
            results["scale2"] = jnp.sum(upstream_cols * branch_cols, axis=0)
            results["down_bias"] = jnp.sum(upstream_cols * layer_scale2, axis=0)
        if chunks - 1 in results and "scaled" not in results:
            grad_lowered1 = out_of_chunks([results[index] for index in range(chunks)])
            row_mean, inv_std1 = stats1[:, 0:1], stats1[:, 1:2]
            normed1 = (flat(pad_rows(tokens_late)).astype(jnp.float32) - row_mean) * inv_std1
            scaled = grad_lowered1 * cols(gain1_late)
            results["scaled"] = (scaled, normed1, inv_std1)
            tasks.add(
                sum_small,
                "row_totals",
                [jnp.sum(scaled, axis=-1), jnp.sum(scaled * normed1, axis=-1)],
                "tensor",
            )
            results["norm1"] = [
                jnp.sum(grad_lowered1 * normed1, axis=0),
                jnp.sum(grad_lowered1, axis=0),
            ]
        if "scale2" in results and "packed2" not in results:
            results["packed2"] = None
            tasks.add(sum_small, "small2", [results["down_bias"], results["scale2"]], "dp")
        if "norm1" in results and "packed" not in results:
            feature_sums = sum(parts[7] for parts in back)
            results["packed"] = None
            small = [
                sum(parts[5] for parts in back)[0],
                sum(parts[6] for parts in back)[0],
                feature_sums[3],
                feature_sums[2],
                feature_sums[0],
                feature_sums[1],
                grad_up_bias,
            ]
            tasks.add(sum_small, "small", small + results["norm1"], "dp")
        if "row_totals" in results and "input_grad" not in results:
            scaled, normed1, inv_std1 = results["scaled"]
            mean_scaled, mean_product = (
                values[:, None] / features for values in results["row_totals"]
            )
            results["input_grad"] = unpad_rows(
                cols(residual_grad) + inv_std1 * (scaled - mean_scaled - normed1 * mean_product)
            )
        if "small" in results and "norm1_sums" not in results:
            results["norm1_sums"] = None
            tasks.add(gather_small, "norm1_all", jnp.stack(results["small"][7:]))

    last = (state, last, tasks.step(last))
    finish(last)
    branch_parts = [
        jnp.dot(activated_late, weight, preferred_element_type=jnp.float32).astype(jnp.bfloat16)
        for weight in split_blocks(after(down_weight, last), 1)
    ]
    tasks.add(scatter_columns, "branch", [branch_parts])

    finished = {}
    last = (last, branch_parts)
    steps = 2 * len(first_order)
    for step in range(steps):
        if step < steps - 3:
            finished["hidden"] = last = hidden_sums.send(last)
        finished["heads"] = last = heads_sums.send(last)
        if tasks.active and step != steps - 5:
            last = (last, tasks.step(last))
            finish(last)
        if step == steps - 2:
            finished["hidden"] = hidden_sums.send(last)
            last = (last, finished["hidden"])
    while tasks.active:
        last = tasks.step(last)
        finish(last)
    grad_down_weight, grad_up_weight = finished["hidden"]
    grad_out_weight, top, bottom = finished["heads"]
    grad_qkv_weight = jnp.concatenate([top, bottom], axis=0)
    (
        grad_query_bias,
        grad_value_bias,
        grad_out_bias,
        grad_layer_scale1,
        grad_norm2_gain,
        grad_norm2_bias,
        grad_up_bias,
        grad_down_bias,
        grad_layer_scale2,
    ) = results["small"][:7] + results["small2"]
    grad_norm1_gain, grad_norm1_bias = results["norm1_all"]
    output, input_grad = results["output"], results["input_grad"]
    return (
        output,
        input_grad,
        grad_norm1_gain,
        grad_norm1_bias,
        grad_qkv_weight,
        grad_query_bias,
        grad_value_bias,
        grad_out_weight,
        grad_out_bias,
        grad_layer_scale1,
        grad_norm2_gain,
        grad_norm2_bias,
        grad_up_weight,
        grad_up_bias,
        grad_down_weight,
        grad_down_bias,
        grad_layer_scale2,
    )


def solution(mesh):
    return jax.shard_map(
        shards,
        mesh=mesh,
        in_specs=(
            P("dp", "tensor"),
            P(),
            P(),
            P(None, "tensor"),
            P("tensor"),
            P("tensor"),
            P("tensor", None),
            P(),
            P(),
            P(),
            P(),
            P(None, "tensor"),
            P("tensor"),
            P("tensor", None),
            P("tensor"),
            P("tensor"),
            P("dp", "tensor"),
        ),
        out_specs=(
            P("dp", "tensor"),
            P("dp", "tensor"),
            P(),
            P(),
            P(None, "tensor"),
            P("tensor"),
            P("tensor"),
            P("tensor", None),
            P(),
            P(),
            P(),
            P(),
            P(None, "tensor"),
            P("tensor"),
            P("tensor", None),
            P("tensor"),
            P("tensor"),
        ),
        check_vma=False,
    )
```

```python
import math

import jax
import jax.numpy as jnp
from jax import lax
from jax.experimental import pallas as pl
from jax.experimental.pallas import tpu as pltpu
from jax.sharding import PartitionSpec as P

HD = 64
TOK_IMG = 257


EPS = 1e-06


def layer_norm(values, gain, bias):
    row_mean = jnp.mean(values, axis=-1, keepdims=True)
    centred = values - row_mean
    inv_std = lax.rsqrt(jnp.mean(centred * centred, axis=-1, keepdims=True) + EPS)
    normed = centred * inv_std
    return (normed, inv_std, normed * gain + bias)


def norm_back(upstream, normed, inv_std, gain):
    scaled = upstream * gain
    return inv_std * (
        scaled
        - jnp.mean(scaled, axis=-1, keepdims=True)
        - normed * jnp.mean(scaled * normed, axis=-1, keepdims=True)
    )


def gelu_parts(hidden_pre):
    cdf_value = 0.5 * (1.0 + jax.scipy.special.erf(hidden_pre * 2.0 ** (-0.5)))
    density = jnp.exp(-0.5 * hidden_pre * hidden_pre) * (2.0 * math.pi) ** (-0.5)
    return (hidden_pre * cdf_value, cdf_value + hidden_pre * density)


def contract_rows(left, right):
    return lax.dot_general(
        left, right, (((0,), (0,)), ((), ())), preferred_element_type=jnp.float32
    )


def contract_cols(left, right):
    return lax.dot_general(
        left, right, (((1,), (1,)), ((), ())), preferred_element_type=jnp.float32
    )


HEAD_COLS = 3 * HD
VMEM_BYTES = 48 << 20


def probs_of(packed, head, keep):
    start = head * HEAD_COLS
    query = packed[:, start : start + HD]
    key = packed[:, start + HD : start + 2 * HD]
    value = packed[:, start + 2 * HD : start + 3 * HD]
    scores = jnp.where(keep, contract_cols(key, query) * HD ** (-0.5), -1e30)
    powers = jnp.exp(scores - jnp.max(scores, axis=0, keepdims=True))
    probs = powers * (1.0 / jnp.sum(powers, axis=0, keepdims=True))
    return query, key, value, probs


def forward_kernel(
    tokens, gain, bias, weight, proj_bias, out_mine, out_theirs, low, packed, mixed, stats, mine,
    theirs,
):
    rows = tokens.shape[1]
    values = tokens[0].astype(jnp.float32)
    _, inv_std, scaled = layer_norm(values, gain[...], bias[...])
    first = lax.broadcasted_iota(jnp.int32, (rows, 128), 1) == 0
    stats[0] = jnp.where(first, jnp.mean(values, axis=-1, keepdims=True), inv_std)
    low[0] = scaled.astype(jnp.bfloat16)
    projected = jnp.dot(low[0], weight[...], preferred_element_type=jnp.float32)
    packed[0] = (projected + proj_bias[...]).astype(jnp.bfloat16)
    keep = lax.broadcasted_iota(jnp.int32, (rows, rows), 0) < TOK_IMG
    columns = packed[0]
    outs = []
    for head in range(weight.shape[1] // HEAD_COLS):
        _, _, value, probs = probs_of(columns, head, keep)
        outs.append(
            jnp.dot(
                value.astype(jnp.float32).T.astype(jnp.bfloat16),
                probs.astype(jnp.bfloat16),
                preferred_element_type=jnp.float32,
            )
        )
    mixed[0] = jnp.concatenate(outs, axis=0).T.astype(jnp.bfloat16)
    for part, out_weight in ((mine, out_mine), (theirs, out_theirs)):
        part[0] = jnp.dot(
            mixed[0], out_weight[...], preferred_element_type=jnp.float32
        ).astype(jnp.bfloat16)


def backward_kernel(
    core, tokens, attended_low, low2_mine, low2_theirs, cotangent, vectors, packed, out_weight,
    back_mine, back_theirs, residual_grad, upstream, grad, mine, theirs, query_sum, value_sum,
    feature_sums,
):
    rows = packed.shape[1]
    heads = packed.shape[2] // HEAD_COLS

    @pl.when(pl.program_id(0) == 0)
    def _():
        query_sum[...] = jnp.zeros_like(query_sum)
        value_sum[...] = jnp.zeros_like(value_sum)
        feature_sums[...] = jnp.zeros_like(feature_sums)

    attended = attended_low[0].astype(jnp.float32) + vectors[0:1]
    residual = tokens[0].astype(jnp.float32) + vectors[1:2] * attended
    normed, inv_std, _ = layer_norm(residual, vectors[2:3], vectors[3:4])
    grad_low2 = rejoin(core[0] == 1, low2_mine, low2_theirs)
    grad_residual = cotangent[0].astype(jnp.float32) + norm_back(
        grad_low2, normed, inv_std, vectors[2:3]
    )
    residual_grad[0] = grad_residual
    grad_attended = grad_residual * vectors[1:2]
    upstream[0] = grad_attended.astype(jnp.bfloat16)
    for row, product in enumerate(
        (grad_low2 * normed, grad_low2, grad_residual * attended, grad_attended)
    ):
        feature_sums[row : row + 1] += jnp.sum(product, axis=0, keepdims=True)
    grad_mixed = contract_cols(upstream[0], out_weight[...]).astype(jnp.bfloat16)
    keep = lax.broadcasted_iota(jnp.int32, (rows, rows), 0) < TOK_IMG
    columns = packed[0]
    queries = []
    for head in range(heads):
        query, key, value, probs = probs_of(columns, head, keep)
        grad_head = grad_mixed[:, head * HD : (head + 1) * HD]
        grad_probs = contract_cols(value, grad_head)
        delta = jnp.sum(probs * grad_probs, axis=0, keepdims=True)
        grad_scores = (probs * (grad_probs - delta) * HD ** (-0.5)).astype(jnp.bfloat16)
        grad_value = jnp.dot(
            probs.astype(jnp.bfloat16), grad_head, preferred_element_type=jnp.float32
        )
        grad_key = jnp.dot(grad_scores, query, preferred_element_type=jnp.float32)
        queries.append(
            jnp.dot(
                key.astype(jnp.float32).T.astype(jnp.bfloat16),
                grad_scores,
                preferred_element_type=jnp.float32,
            )
        )
        start = head * HEAD_COLS
        grad[0, :, start + HD : start + 2 * HD] = grad_key.astype(jnp.bfloat16)
        grad[0, :, start + 2 * HD : start + 3 * HD] = grad_value.astype(jnp.bfloat16)
        value_sum[:, head * HD : (head + 1) * HD] += jnp.sum(grad_value, axis=0, keepdims=True)
    grad_query = jnp.concatenate(queries, axis=0).T
    query_sum[...] += jnp.sum(grad_query, axis=0, keepdims=True)
    for head in range(heads):
        start = head * HEAD_COLS
        grad[0, :, start : start + HD] = grad_query[:, head * HD : (head + 1) * HD].astype(
            jnp.bfloat16
        )
    for part, weight in ((mine, back_mine), (theirs, back_theirs)):
        part[0] = contract_cols(grad[0], weight[...]).astype(jnp.bfloat16)


def rejoin(upper, mine, theirs):
    own, other = mine[0].astype(jnp.float32), theirs[0].astype(jnp.float32)
    return jnp.concatenate(
        [jnp.where(upper, other, own), jnp.where(upper, own, other)], axis=-1
    )


def hidden_kernel(
    core, tokens, mine, theirs, upstream, vectors, up_weight, up_bias, down_weight, up_mine,
    up_theirs, attended_low, low, activated_low, branch_grad, grad_low, part_mine, part_theirs,
    bias_sum,
):
    @pl.when(pl.program_id(0) == 0)
    def _():
        bias_sum[...] = jnp.zeros_like(bias_sum)

    joined = rejoin(core[0] == 1, mine, theirs)
    attended_low[0] = joined.astype(jnp.bfloat16)
    residual = tokens[0].astype(jnp.float32) + vectors[1:2] * (joined + vectors[0:1])
    _, _, scaled = layer_norm(residual, vectors[2:3], vectors[3:4])
    low[0] = scaled.astype(jnp.bfloat16)
    branch_grad[0] = (upstream[0].astype(jnp.float32) * vectors[4:5]).astype(jnp.bfloat16)
    hidden_pre = jnp.dot(low[0], up_weight[...], preferred_element_type=jnp.float32) + up_bias[...]
    activated, slope = gelu_parts(hidden_pre)
    activated_low[0] = activated.astype(jnp.bfloat16)
    grad_pre = contract_cols(branch_grad[0], down_weight[...]) * slope
    bias_sum[...] += jnp.sum(grad_pre, axis=0, keepdims=True)
    grad_low[0] = grad_pre.astype(jnp.bfloat16)
    for part, weight in ((part_mine, up_mine), (part_theirs, up_theirs)):
        part[0] = contract_cols(grad_low[0], weight[...]).astype(jnp.bfloat16)


def run_images(kernel, base, args, outs, name, core=None, carried=()):
    images, total = args[0].shape[0], max(out.shape[0] for out in outs if len(out.shape) == 3)

    def spec(shape):
        if len(shape) == 2:
            return pl.BlockSpec(shape, lambda image: (0, 0))
        first = base if shape[0] == total else 0
        return pl.BlockSpec((1,) + shape[1:], lambda image: (image + first, 0, 0))

    in_specs = [spec(arg.shape) for arg in args]
    if core is not None:
        in_specs = [pl.BlockSpec(memory_space=pltpu.SMEM)] + in_specs
        args = (core,) + tuple(args)
    skipped, count = len(carried), len(args)

    def body(*refs):
        kernel(*refs[:count], *refs[count + skipped :])

    return pl.pallas_call(
        body,
        grid=(images,),
        in_specs=in_specs + [pl.BlockSpec(memory_space=pl.ANY)] * skipped,
        out_specs=[spec(out.shape) for out in outs],
        out_shape=outs,
        input_output_aliases={count + index: index for index in range(skipped)},
        compiler_params=pltpu.CompilerParams(vmem_limit_bytes=VMEM_BYTES),
        name=name,
    )(*args, *carried)


def low_of(images, rows, width):
    return jax.ShapeDtypeStruct((images, rows, width), jnp.bfloat16)


def total_of(rows, width):
    return jax.ShapeDtypeStruct((rows, width), jnp.float32)


def attention_forward(total, base, carried, tokens, gain, bias, weight, *args):
    chunk, rows, features = tokens.shape
    out_mine = args[1]
    half = out_mine.shape[1]
    widths = (features, weight.shape[1], out_mine.shape[0])
    outs = [low_of(total, rows, width) for width in widths]
    outs += [jax.ShapeDtypeStruct((total, rows, 128), jnp.float32)]
    outs += [low_of(chunk, rows, half), low_of(chunk, rows, half)]
    args = (tokens, gain, bias, weight) + args
    return run_images(forward_kernel, base, args, outs, "attention_forward", None, carried)


def hidden_both(total, base, carried, core, tokens, mine, *args):
    chunk, rows, features = tokens.shape
    units, half = args[3].shape[1], mine.shape[2]
    widths = (features, features, units, features, units)
    outs = [low_of(total, rows, width) for width in widths]
    outs += [low_of(chunk, rows, half), low_of(chunk, rows, half), total_of(1, units)]
    args = (tokens, mine) + args
    return run_images(hidden_kernel, base, args, outs, "hidden_both", core, carried)


def attention_backward(total, base, carried, core, tokens, *args):
    chunk, rows, features = tokens.shape
    width, half = args[5].shape[2], args[7].shape[0]
    outs = [jax.ShapeDtypeStruct((total, rows, features), jnp.float32)]
    outs += [low_of(total, rows, columns) for columns in (features, width)]
    outs += [low_of(chunk, rows, half), low_of(chunk, rows, half)]
    outs += [total_of(1, width // 3), total_of(1, width // 3), total_of(4, features)]
    args = (tokens,) + args
    return run_images(backward_kernel, base, args, outs, "attention_backward", core, carried)


def exchange(block, axis, bit):
    size = lax.axis_size(axis)
    return lax.ppermute(block, axis, [(index, index ^ (1 << bit)) for index in range(size)])


def bit_of(axis, bit):
    return (lax.axis_index(axis) >> bit) % 2 == 1


def bits_in(axis):
    return (lax.axis_size(axis) - 1).bit_length()


def after(value, *others):
    return lax.optimization_barrier((value, *others))[0]


def split_blocks(values, dim):
    count = lax.axis_size("tensor")
    blocks = jnp.split(values, count, axis=dim)
    even = jnp.concatenate(blocks[0::2], axis=dim)
    odd = jnp.concatenate(blocks[1::2], axis=dim)
    upper = bit_of("tensor", 0)
    return jnp.where(upper, odd, even), jnp.where(upper, even, odd)


def split_halves(values, dim):
    low, high = jnp.split(values, 2, axis=dim)
    upper = bit_of("tensor", 0)
    return jnp.where(upper, high, low), jnp.where(upper, low, high)


def join_blocks(mine, theirs):
    count = lax.axis_size("tensor") // 2
    upper = bit_of("tensor", 0)
    pieces = []
    for own, other in zip(jnp.split(mine, count, axis=-1), jnp.split(theirs, count, axis=-1)):
        pieces += [jnp.where(upper, other, own), jnp.where(upper, own, other)]
    return jnp.concatenate(pieces, axis=-1)


def gather_far(block, others=()):
    for bit in range(1, bits_in("tensor")):
        got = after(exchange(block, "tensor", bit), others)
        upper = bit_of("tensor", bit)
        block = jnp.concatenate(
            [jnp.where(upper, got, block), jnp.where(upper, block, got)], axis=-1
        )
    return block


def gather_near(block):
    return join_blocks(block, exchange(block, "tensor", 0))


def add_near(mine, theirs, others=()):
    got = after(exchange(theirs, "tensor", 0), others)
    return (mine.astype(jnp.float32) + got.astype(jnp.float32)).astype(jnp.bfloat16)


def add_far(total, others=()):
    for bit in range(1, bits_in("tensor")):
        got = after(exchange(total, "tensor", bit), others)
        total = (total.astype(jnp.float32) + got.astype(jnp.float32)).astype(jnp.bfloat16)
    return total


def pick(terms, upper):
    halves = [jnp.split(term, 2, axis=0) for term in terms]
    return sum(jnp.where(upper, high, low).astype(jnp.float32) for low, high in halves)


def double_join(grad, got, bit):
    upper = bit_of("dp", bit)
    return jnp.concatenate([jnp.where(upper, got, grad), jnp.where(upper, grad, got)], axis=0)


def row_sums(name, flows):
    steps = len(flows[0][1])
    grads = [(grad, order) for group, order in flows for grad in group]
    orders = [order for _, order in grads]
    terms = [(grad,) for grad, _ in grads]
    for step in range(steps):
        uppers = [bit_of("dp", order[step]) for order in orders]
        sent = [
            pick(sums, jnp.logical_not(upper)).astype(jnp.bfloat16)
            for sums, upper in zip(terms, uppers)
        ]
        with jax.named_scope(f"{name}_halves_{step}"):
            got = [exchange(part, "dp", order[step]) for part, order in zip(sent, orders)]
        others = yield sent
        got = lax.optimization_barrier((got, others))[0]
        terms = [(pick(sums, upper), part) for sums, upper, part in zip(terms, uppers, got)]
    blocks = [sum(term.astype(jnp.float32) for term in sums) for sums in terms]
    blocks = [block.astype(jnp.bfloat16) for block in blocks]
    for step in reversed(range(steps)):
        with jax.named_scope(f"{name}_doubles_{step}"):
            got = [exchange(block, "dp", order[step]) for block, order in zip(blocks, orders)]
        others = yield blocks
        got = lax.optimization_barrier((got, others))[0]
        blocks = [
            double_join(block, part, order[step])
            for block, part, order in zip(blocks, got, orders)
        ]
    yield [block.astype(jnp.float32) for block in blocks]


def scatter_columns(results, name, parts):
    got = yield [exchange(theirs, "tensor", 0) for _, theirs in parts]
    totals = [
        flat(mine).astype(jnp.float32) + flat(part).astype(jnp.float32)
        for (mine, _), part in zip(parts, got)
    ]
    for bit in reversed(range(1, bits_in("tensor"))):
        upper = bit_of("tensor", bit)
        halves = [jnp.split(total, 2, axis=-1) for total in totals]
        got = yield [
            exchange(jnp.where(upper, low, high).astype(jnp.bfloat16), "tensor", bit)
            for low, high in halves
        ]
        totals = [
            jnp.where(upper, high, low) + part.astype(jnp.float32)
            for (low, high), part in zip(halves, got)
        ]
    results[name] = jnp.concatenate(totals, axis=0)


def sum_small(results, name, values, axis):
    sizes = [value.shape[0] for value in values]
    starts = [sum(sizes[:index]) for index in range(len(sizes))]
    packed = sum(
        jnp.pad(value, (start, sum(sizes) - start - size))
        for value, start, size in zip(values, starts, sizes)
    )
    for bit in range(bits_in(axis)):
        (got,) = yield [exchange(packed, axis, bit)]
        packed = packed + got
    sums, start = [], 0
    for value in values:
        sums.append(packed[start : start + value.shape[0]])
        start += value.shape[0]
    results[name] = sums


def gather_small(results, name, block):
    for bit in range(1, bits_in("tensor")):
        (got,) = yield [exchange(block, "tensor", bit)]
        upper = bit_of("tensor", bit)
        block = jnp.concatenate(
            [jnp.where(upper, got, block), jnp.where(upper, block, got)], axis=-1
        )
    (got,) = yield [exchange(block, "tensor", 0)]
    results[name] = join_blocks(block, got)


def flat(values):
    return values.reshape(-1, values.shape[-1])


class Tasks:
    def __init__(self):
        self.results, self.active = {}, []

    def add(self, task, name, *args):
        chain = task(self.results, name, *args)
        self.active.append((chain, next(chain)))

    def step(self, others):
        got = lax.optimization_barrier(([wanted for _, wanted in self.active], others))[0]
        chains, self.active = [chain for chain, _ in self.active], []
        for chain, arrived in zip(chains, got):
            try:
                self.active.append((chain, chain.send(arrived)))
            except StopIteration:
                pass
        return got


def shards(
    tokens,
    norm1_gain,
    norm1_bias,
    qkv_weight,
    query_bias,
    value_bias,
    out_weight,
    out_bias,
    layer_scale1,
    norm2_gain,
    norm2_bias,
    up_weight,
    up_bias,
    down_weight,
    down_bias,
    layer_scale2,
    cotangent,
):
    images = tokens.shape[0] // TOK_IMG
    width_local = tokens.shape[1]
    features = norm1_gain.shape[0]
    padded = -(-TOK_IMG // 8) * 8
    heads_local = query_bias.shape[0] // HD
    chunks = 2 if images % 2 == 0 else 1
    col_start = lax.axis_index("tensor") * width_local

    def cols(values):
        return lax.dynamic_slice_in_dim(values, col_start, width_local, values.ndim - 1)

    def pad_rows(values):
        values = values.reshape(images, TOK_IMG, width_local)
        return jnp.pad(values, ((0, 0), (0, padded - TOK_IMG), (0, 0)))

    def unpad_rows(values):
        values = values.reshape(images, padded, width_local)
        return values[:, :TOK_IMG].reshape(images * TOK_IMG, width_local)

    def in_chunks(values):
        return jnp.split(values, chunks, axis=0)

    def out_of_chunks(values):
        return jnp.concatenate(values, axis=0)

    count = images // chunks
    core = (lax.axis_index("tensor") % 2).astype(jnp.int32).reshape(1)
    proj_bias = jnp.stack(
        [
            query_bias.reshape(heads_local, HD),
            jnp.zeros((heads_local, HD), jnp.float32),
            value_bias.reshape(heads_local, HD),
        ],
        axis=1,
    ).reshape(1, 3 * heads_local * HD)
    tokens_given, cotangent_given = tokens, cotangent
    tokens = pad_rows(tokens)
    cotangent = pad_rows(cotangent)
    token_parts = in_chunks(tokens)
    out_mine, out_theirs = split_halves(out_weight, 1)
    up_mine, up_theirs = split_halves(up_weight, 0)
    qkv_mine, qkv_theirs = split_blocks(qkv_weight, 0)
    out_mine, out_theirs = after((out_mine, out_theirs), (up_mine, up_theirs, qkv_mine, qkv_theirs))
    far = gather_far(token_parts[0])
    scale2_sent, rest_sent = after(
        (layer_scale2, jnp.concatenate(token_parts[1:] + [cotangent], axis=0)), far
    )
    scale2_far = scale2_sent[None]
    whole, forward, carried, attended, sums, given = [], [], (), [], [], ()
    for index in range(chunks):
        joined = gather_near(far if index == 0 else rest_far[(index - 1) * count : index * count])
        whole.append(after(joined, attended))
        parts = attention_forward(
            images,
            index * count,
            carried,
            whole[index],
            norm1_gain[None],
            norm1_bias[None],
            qkv_weight,
            proj_bias,
            out_mine,
            out_theirs,
        )
        if index == 0:
            scale2_far = gather_far(scale2_far, parts[4])
            rest_far = gather_far(rest_sent, parts[4:6])
            cotangent_far = rest_far[images - count :]
        carried, given = parts[:4], parts[4:6]
        forward.append(parts)
        if index > 0:
            sums.append(add_far(attended[index - 1], given))
            given = after(given, sums[-1])
        attended.append(add_near(*given))
    packed = carried[1]
    lowered1, mixed, stats1 = flat(carried[0]), flat(carried[2]), flat(carried[3])
    scale2_far = after(scale2_far, forward[-1][4])
    upstream = gather_near(after(cotangent_far, forward[-1][4]))
    scale2_all = gather_near(scale2_far)
    vectors = jnp.concatenate(
        [out_bias[None], layer_scale1[None], norm2_gain[None], norm2_bias[None], scale2_all]
    )

    hidden, carried, low2, given = [], (), [], (vectors, upstream)
    for index in range(chunks):
        if index == chunks - 1:
            sums.append(add_far(attended[index], given))
        mine = sums[index]
        theirs = exchange(mine, "tensor", 0)
        parts = hidden_both(
            images,
            index * count,
            carried,
            core,
            whole[index],
            after(mine, low2),
            theirs,
            upstream,
            vectors,
            up_weight,
            up_bias[None],
            down_weight,
            up_mine,
            up_theirs,
        )
        carried, given = parts[:5], parts[5:7]
        hidden.append(parts)
        if index < chunks - 1:
            low2.append(add_near(*given))
    attended_low = carried[0]
    lowered2, activated_low, branch_grad, grad_pre_low = (flat(part) for part in carried[1:])
    grad_up_bias = sum(parts[7] for parts in hidden)[0]
    grad_down_weight = contract_rows(activated_low, branch_grad)
    low2.append(add_near(*given, grad_down_weight))
    low2_sums = [add_far(low2[0], low2[-1:])]
    low2_theirs = [exchange(low2_sums[0], "tensor", 0)]
    grad_up_weight = contract_rows(after(lowered2, low2_sums), grad_pre_low)
    first_order = tuple(range(bits_in("dp")))
    second_order = first_order[1:2] + first_order[:1] + first_order[2:]
    hidden_sums = row_sums(
        "hidden", [([grad_down_weight], first_order), ([grad_up_weight], second_order)]
    )
    sent = next(hidden_sums)

    tasks = Tasks()
    results = tasks.results
    back, carried, given = [], (), sent
    for index in range(chunks):
        if index > 0:
            low2_sums.append(add_far(low2[index], given))
            low2_theirs.append(exchange(low2_sums[index], "tensor", 0))
        mine, theirs = after((low2_sums[index], low2_theirs[index]), given)
        parts = attention_backward(
            images,
            index * count,
            carried,
            core,
            whole[index],
            attended_low,
            mine,
            theirs,
            upstream,
            vectors,
            packed,
            out_weight,
            qkv_mine,
            qkv_theirs,
        )
        carried, given = parts[:3], parts[3:5]
        back.append(parts)
        tasks.add(scatter_columns, index, [given])
    residual_grad, grad_attended, grad_projected = (flat(part) for part in carried)
    state = hidden_sums.send(given)
    state = (state, tasks.step(state))
    grad_attended, grad_projected = after((grad_attended, grad_projected), state)
    grad_out_weight = contract_rows(mixed, grad_attended)
    grad_qkv_weight = contract_rows(lowered1, grad_projected)
    state = hidden_sums.send((grad_out_weight, grad_qkv_weight))
    rows = grad_qkv_weight.shape[0]
    first_rows = 3 * rows // 8
    grad_out_weight, grad_qkv_weight = after((grad_out_weight, grad_qkv_weight), state)
    heads_sums = row_sums(
        "heads",
        [
            ([grad_out_weight, grad_qkv_weight[:first_rows]], first_order),
            ([grad_qkv_weight[first_rows:]], second_order),
        ],
    )
    last = next(heads_sums)
    late = after(
        (tokens_given, cotangent_given, norm1_gain, layer_scale1, out_bias, activated_low), last
    )
    tokens_late, cotangent_late, gain1_late, scale1_late, out_bias_late, activated_late = late
    def finish(others):
        if "branch" in results and "output" not in results:
            branch_cols = results["branch"] + down_bias
            own, upstream_own = flat(pad_rows(tokens_late)), flat(pad_rows(cotangent_late))
            attended_cols = cols(flat(attended_low)).astype(jnp.float32) + cols(out_bias_late)
            residual_cols = own.astype(jnp.float32) + cols(scale1_late) * attended_cols
            results["output"] = unpad_rows(residual_cols + layer_scale2 * branch_cols)
            upstream_cols = upstream_own.astype(jnp.float32)
            results["scale2"] = jnp.sum(upstream_cols * branch_cols, axis=0)
            results["down_bias"] = jnp.sum(upstream_cols * layer_scale2, axis=0)
        if chunks - 1 in results and "scaled" not in results:
            grad_lowered1 = out_of_chunks([results[index] for index in range(chunks)])
            row_mean, inv_std1 = stats1[:, 0:1], stats1[:, 1:2]
            normed1 = (flat(pad_rows(tokens_late)).astype(jnp.float32) - row_mean) * inv_std1
            scaled = grad_lowered1 * cols(gain1_late)
            results["scaled"] = (scaled, normed1, inv_std1)
            tasks.add(
                sum_small,
                "row_totals",
                [jnp.sum(scaled, axis=-1), jnp.sum(scaled * normed1, axis=-1)],
                "tensor",
            )
            results["norm1"] = [
                jnp.sum(grad_lowered1 * normed1, axis=0),
                jnp.sum(grad_lowered1, axis=0),
            ]
        if "scale2" in results and "packed2" not in results:
            results["packed2"] = None
            tasks.add(sum_small, "small2", [results["down_bias"], results["scale2"]], "dp")
        if "norm1" in results and "packed" not in results:
            feature_sums = sum(parts[7] for parts in back)
            results["packed"] = None
            small = [
                sum(parts[5] for parts in back)[0],
                sum(parts[6] for parts in back)[0],
                feature_sums[3],
                feature_sums[2],
                feature_sums[0],
                feature_sums[1],
                grad_up_bias,
            ]
            tasks.add(sum_small, "small", small + results["norm1"], "dp")
        if "row_totals" in results and "input_grad" not in results:
            scaled, normed1, inv_std1 = results["scaled"]
            mean_scaled, mean_product = (
                values[:, None] / features for values in results["row_totals"]
            )
            results["input_grad"] = unpad_rows(
                cols(residual_grad) + inv_std1 * (scaled - mean_scaled - normed1 * mean_product)
            )
        if "small" in results and "norm1_sums" not in results:
            results["norm1_sums"] = None
            tasks.add(gather_small, "norm1_all", jnp.stack(results["small"][7:]))

    last = (state, last, tasks.step(last))
    finish(last)
    branch_parts = [
        jnp.dot(activated_late, weight, preferred_element_type=jnp.float32).astype(jnp.bfloat16)
        for weight in split_blocks(after(down_weight, last), 1)
    ]
    tasks.add(scatter_columns, "branch", [branch_parts])

    finished = {}
    last = (last, branch_parts)
    steps = 2 * len(first_order)
    for step in range(steps):
        if step < steps - 4:
            finished["hidden"] = last = hidden_sums.send(last)
        finished["heads"] = last = heads_sums.send(last)
        if step == steps - 4:
            finished["hidden"] = last = hidden_sums.send(last)
        if tasks.active and step != steps - 5:
            last = (last, tasks.step(last))
            finish(last)
        if step == steps - 2:
            finished["hidden"] = hidden_sums.send(last)
            last = (last, finished["hidden"])
    while tasks.active:
        last = tasks.step(last)
        finish(last)
    grad_down_weight, grad_up_weight = finished["hidden"]
    grad_out_weight, top, bottom = finished["heads"]
    grad_qkv_weight = jnp.concatenate([top, bottom], axis=0)
    (
        grad_query_bias,
        grad_value_bias,
        grad_out_bias,
        grad_layer_scale1,
        grad_norm2_gain,
        grad_norm2_bias,
        grad_up_bias,
        grad_down_bias,
        grad_layer_scale2,
    ) = results["small"][:7] + results["small2"]
    grad_norm1_gain, grad_norm1_bias = results["norm1_all"]
    output, input_grad = results["output"], results["input_grad"]
    return (
        output,
        input_grad,
        grad_norm1_gain,
        grad_norm1_bias,
        grad_qkv_weight,
        grad_query_bias,
        grad_value_bias,
        grad_out_weight,
        grad_out_bias,
        grad_layer_scale1,
        grad_norm2_gain,
        grad_norm2_bias,
        grad_up_weight,
        grad_up_bias,
        grad_down_weight,
        grad_down_bias,
        grad_layer_scale2,
    )


def solution(mesh):
    return jax.shard_map(
        shards,
        mesh=mesh,
        in_specs=(
            P("dp", "tensor"),
            P(),
            P(),
            P(None, "tensor"),
            P("tensor"),
            P("tensor"),
            P("tensor", None),
            P(),
            P(),
            P(),
            P(),
            P(None, "tensor"),
            P("tensor"),
            P("tensor", None),
            P("tensor"),
            P("tensor"),
            P("dp", "tensor"),
        ),
        out_specs=(
            P("dp", "tensor"),
            P("dp", "tensor"),
            P(),
            P(),
            P(None, "tensor"),
            P("tensor"),
            P("tensor"),
            P("tensor", None),
            P(),
            P(),
            P(),
            P(),
            P(None, "tensor"),
            P("tensor"),
            P("tensor", None),
            P("tensor"),
            P("tensor"),
        ),
        check_vma=False,
    )
```
